256 devices in a mesh: mic: 8 (over x, core), bin: 32 (over z, y).
Axes of the slice: x: 4, y: 4, z: 8, core: 2. Of those that a mesh axis runs over, the one named last changes fastest.
Arguments:
- images: bfloat16 [1024, 256, 256], P(('mic', 'bin')), may hold values from -6 to 6
- offsets: int32 [2, 1024], P(None, ('mic', 'bin')), may hold values from 0 to 255
- ctf_group: int32 [1024], P(('mic', 'bin')), may hold values from 0 to 63
- particle_bin: int32 [1024], P(('mic', 'bin')), may hold values from 0 to 2047, as said below
- bin_place: int32 [2048], replicated, may hold values from 0 to 2047, as said below
- defocus: float32 [64], replicated, may hold values from 40 to 160
- bfactor: float32 [64], replicated, may hold values from 0.2 to 2
- references: bfloat16 [2048, 256, 256], P(('mic', 'bin')), may hold values from -6 to 6
Outputs:
- refined: bfloat16 [2048, 256, 256], P(('mic', 'bin'))
- scores: float32 [1024], P(('mic', 'bin'))
The draws below stay inside these ranges and needn't reach their ends.
Inputs may be any that keep to these rules, and one draw needn't show every extreme that they name: bin_place is a permutation. A particle's owner is bin_place[particle_bin] // 8, with bin index owner % 32 and mic index owner // 32. Of the 4 particles of one device, at most 1 have owners with one bin index, and some device of every mic row reaches it. `particle_bin`: within one mic row exactly 4 particles have owners with each bin index, and at most 1 have the same owner; in every mic row some owner has exactly 1. Several particles may share one bin.
All inputs are finite; a program needn't handle non-finite values.
Results may differ from the reference program's by a relative error of at most 0.0055.
Values may be sent and summed in bfloat16 or wider, within the bound.
A program may use at most 64 MiB of HBM per device.

```python
import math
import jax
import jax.numpy as jnp
from jax import lax

IMAGE_SIDE = 256
PARTICLE_DEV = 4
BIN_DEV = 8
CTF_GROUPS = 64
ITERS = 2
PARTICLES = 1024
BINS = 2048
N_MIC = 8
N_BIN = 32


def routing(key):
    cap_first = (PARTICLE_DEV + N_BIN - 1) // N_BIN
    cap_second = (3 * PARTICLE_DEV + 2 * N_MIC - 1) // (2 * N_MIC)
    first_slots = N_BIN * cap_first
    second_slots = N_MIC * cap_second
    key_forced = jax.random.fold_in(key, 101)
    key_order = jax.random.fold_in(key, 102)
    key_mic = jax.random.fold_in(key, 103)
    key_second = jax.random.fold_in(key, 104)
    key_local = jax.random.fold_in(key, 105)
    key_other = jax.random.fold_in(key, 106)
    key_perm = jax.random.fold_in(key, 107)
    key_half = jax.random.fold_in(key, 108)
    slot_ids = jnp.arange(first_slots, dtype=jnp.int32)
    forced_bin = jax.random.randint(key_forced, (N_MIC, 1), 0, N_BIN)
    half_row = jax.random.randint(key_half, (), 0, N_MIC)
    row_ids = jnp.arange(N_MIC, dtype=jnp.int32)[:, None]
    forced_bin = jnp.where(row_ids == half_row, N_BIN // 2, forced_bin)
    scores_first = jax.random.randint(key_order, (N_MIC, first_slots), 0, 1 << 16) * first_slots + slot_ids[None, :]
    scores_first = jnp.where(slot_ids[None, :] // cap_first == forced_bin, slot_ids[None, :] - first_slots, scores_first)
    chosen = jnp.argsort(scores_first, axis=1)[:, :PARTICLE_DEV]
    rotation = chosen // cap_first
    device_ids = jnp.arange(N_BIN, dtype=jnp.int32)
    target_bin = (device_ids[None, :, None] + rotation[:, None, :]) % N_BIN
    mic_ids = jnp.arange(second_slots, dtype=jnp.int32)
    forced_mic = jax.random.randint(key_mic, (N_MIC, N_BIN, 1), 0, N_MIC)
    scores_second = jax.random.randint(key_second, (N_MIC, N_BIN, second_slots), 0, 1 << 16) * second_slots + mic_ids
    scores_second = jnp.where(mic_ids // cap_second == forced_mic, mic_ids - second_slots, scores_second)
    mic_slot = jnp.argsort(scores_second, axis=2)[:, :, :PARTICLE_DEV] // cap_second
    target_mic = jnp.take_along_axis(mic_slot, target_bin, axis=1)
    local_one = jax.random.randint(key_local, (N_MIC, N_BIN, PARTICLE_DEV), 0, BIN_DEV)
    local_two = jax.random.randint(key_other, (N_MIC, N_BIN, PARTICLE_DEV), 0, BIN_DEV)
    local_bin = jnp.minimum(local_one, local_two)
    places = ((target_mic * N_BIN + target_bin) * BIN_DEV + local_bin).reshape(-1)
    bin_scores = jax.random.randint(key_perm, (BINS,), 0, 1 << 12) * BINS + jnp.arange(BINS, dtype=jnp.int32)
    bin_place = jnp.argsort(bin_scores).astype(jnp.int32)
    bin_at_place = jnp.argsort(bin_place).astype(jnp.int32)
    particle_bin = jnp.take(bin_at_place, places).astype(jnp.int32)
    return (bin_place, particle_bin)


def draw_bin_place(key, part):
    return routing(key)[0]


def draw_particle_bin(key, part):
    return routing(key)[1]


def touch_ends(drawn, own_key, low, top_value):
    extent = drawn.shape
    place = [jax.random.randint(jax.random.fold_in(own_key, axis), (), 0, extent[axis]) for axis in range(len(extent))]
    drawn = drawn.at[tuple(place)].set(low)
    longest = extent.index(max(extent))
    place[longest] = (place[longest] + 1) % extent[longest]
    return drawn.at[tuple(place)].set(top_value)


def steps_of(rng, shape, pieces, smallest, high):
    def one(dim, parts):
        steps = jax.random.uniform(jax.random.fold_in(jax.random.fold_in(rng, 6), dim), (parts,), jnp.float32, smallest / len(pieces), high / len(pieces))
        return jnp.repeat(jnp.exp(steps), shape[dim] // parts).reshape((-1,) + (1,) * (len(shape) - dim - 1))

    factor_of = one(*pieces[0])
    for cut in pieces[1:]:
        factor_of = factor_of * one(*cut)
    return factor_of


def noise(key, extent, width, most, pieces=(), held_as=jnp.bfloat16):
    drawn = jax.random.normal(key, extent, jnp.float32) * width
    if len(pieces) > 0:
        drawn = steps_of(key, extent, pieces, -0.22, 0.18) * drawn
    return jnp.clip(drawn, min=-most, max=most).astype(held_as)


def setup_inputs(seed: int = 0) -> dict:
    seeds = jax.random.split(jax.random.key(seed), 9)
    return {
        "images": noise(seeds[0], (PARTICLES, IMAGE_SIDE, IMAGE_SIDE), 1.0, 6.0, ((0, 256),)),
        "offsets": touch_ends(jax.random.randint(seeds[1], (2, PARTICLES), 0, IMAGE_SIDE), jax.random.fold_in(seeds[1], 1), 0, IMAGE_SIDE - 1).astype(jnp.int32),
        "ctf_group": touch_ends(jax.random.randint(seeds[2], (PARTICLES,), 0, CTF_GROUPS), jax.random.fold_in(seeds[2], 1), 0, CTF_GROUPS - 1).astype(jnp.int32),
        "particle_bin": draw_particle_bin(jax.random.fold_in(seeds[8], 71), 0),
        "bin_place": draw_bin_place(jax.random.fold_in(seeds[8], 71), 0),
        "defocus": jnp.clip(jnp.exp(jax.random.uniform(seeds[5], (CTF_GROUPS,), jnp.float32, math.log(40.0), math.log(160.0))), 40.0, 160.0),
        "bfactor": jnp.clip(jnp.exp(jax.random.uniform(seeds[6], (CTF_GROUPS,), jnp.float32, math.log(0.2), math.log(2.0))), 0.2, 2.0),
        "references": noise(seeds[7], (BINS, IMAGE_SIDE, IMAGE_SIDE), 1.0, 6.0, ((0, 256),)),
    }


PRIOR_WEIGHT = 0.5
EPSILON = 1e-06
CONTRAST = 0.1
AMPLITUDE = math.sqrt(1.0 - CONTRAST * CONTRAST)

def hartley(image_side):
    row_index = lax.broadcasted_iota(jnp.int32, (image_side, image_side), 0)
    column_index = lax.broadcasted_iota(jnp.int32, (image_side, image_side), 1)
    phases = row_index * column_index % image_side
    angles = phases.astype(jnp.float32) * (2.0 * math.pi / image_side)
    return ((jnp.cos(angles) + jnp.sin(angles)) / math.sqrt(image_side)).astype(jnp.bfloat16)

def radius_square(image_side):
    frequency = jnp.arange(image_side, dtype=jnp.int32)
    folded = jnp.minimum(frequency, image_side - frequency).astype(jnp.float32)
    nyquist = image_side / 2.0
    square = (folded[:, None] * folded[:, None] + folded[None, :] * folded[None, :]) / (nyquist * nyquist)
    return square.reshape(image_side * image_side)

def ctf_rows(focus, damping, image_side):
    radial = radius_square(image_side)
    aberration = focus[:, None] * radial[None, :]
    envelope = jnp.exp(-damping[:, None] * radial[None, :])
    return -(AMPLITUDE * jnp.sin(aberration) + CONTRAST * jnp.cos(aberration)) * envelope

def shifted(picture, shift_pair):
    image_side = picture.shape[0]
    doubled = jnp.concatenate([picture, picture], axis=0)
    rows_moved = lax.dynamic_slice_in_dim(doubled, shift_pair[0], image_side, 0)
    doubled = jnp.concatenate([rows_moved, rows_moved], axis=1)
    return lax.dynamic_slice_in_dim(doubled, shift_pair[1], image_side, 1)

def compare(ref_rows, ctf_table, spectra, image_side):
    predicted = ctf_table * ref_rows.astype(jnp.float32)
    values = spectra.astype(jnp.float32)
    cross_term = lax.optimization_barrier(jnp.mean(predicted * values, axis=1))
    model_power = lax.optimization_barrier(jnp.mean(predicted * predicted, axis=1)) + EPSILON
    data_power = lax.optimization_barrier(jnp.mean(values * values, axis=1)) + EPSILON
    correlation = cross_term / jnp.sqrt(model_power * data_power)
    weights = jax.nn.sigmoid(image_side * correlation).astype(jnp.bfloat16)
    weighted = (weights.astype(jnp.float32)[:, None] * ctf_table * values).astype(jnp.bfloat16)
    return (correlation, weights, weighted)

def reference(images, offsets, ctf_group, particle_bin, bin_place, defocus, bfactor, references):
    blocks = PARTICLES // PARTICLE_DEV
    pixel_count = IMAGE_SIDE * IMAGE_SIDE
    basis = lax.optimization_barrier(hartley(IMAGE_SIDE)).astype(jnp.float32)

    def spectra_block(inputs):
        pictures, shift_pairs = inputs
        moved = jax.vmap(shifted)(pictures, shift_pairs).astype(jnp.float32)
        partial_rows = jnp.einsum('kx,pxy->pky', basis, moved).astype(jnp.bfloat16)
        partial_rows = lax.optimization_barrier(partial_rows).astype(jnp.float32)
        return jnp.einsum('pky,ly->pkl', partial_rows, basis).astype(jnp.bfloat16)
    spectra = lax.map(spectra_block, (images.reshape(blocks, PARTICLE_DEV, IMAGE_SIDE, IMAGE_SIDE), offsets.T.reshape(blocks, PARTICLE_DEV, 2)))
    spectra = spectra.reshape(blocks, PARTICLE_DEV, pixel_count)
    places = bin_place[particle_bin].astype(jnp.int32).reshape(blocks, PARTICLE_DEV)
    focus = defocus[ctf_group].reshape(blocks, PARTICLE_DEV)
    damping = bfactor[ctf_group].reshape(blocks, PARTICLE_DEV)
    current = references.reshape(BINS, pixel_count)
    scores = jnp.zeros((PARTICLES,), jnp.float32)
    for iteration in range(ITERS):
        frozen = current

        def one_block(carry, inputs):
            numerator, denominator = carry
            block_spectra, block_places, block_focus, block_damping = inputs
            ctf_table = ctf_rows(block_focus, block_damping, IMAGE_SIDE)
            ref_rows = frozen[block_places]
            correlation, weights, weighted = compare(ref_rows, ctf_table, block_spectra, IMAGE_SIDE)
            numerator = numerator.at[block_places].add(weighted.astype(jnp.float32))
            denominator = denominator.at[block_places].add(weights.astype(jnp.float32)[:, None] * ctf_table * ctf_table)
            return ((numerator, denominator), correlation)
        start = (jnp.zeros((BINS, pixel_count), jnp.float32), jnp.zeros((BINS, pixel_count), jnp.float32))
        (numerator, denominator), correlation = lax.scan(one_block, start, (spectra, places, focus, damping))
        current = ((numerator + PRIOR_WEIGHT * frozen.astype(jnp.float32)) / (denominator + PRIOR_WEIGHT)).astype(jnp.bfloat16)
        scores = correlation.reshape(PARTICLES)
    return (current.reshape(BINS, IMAGE_SIDE, IMAGE_SIDE), scores)
```

```python
import functools
import math

import jax
import jax.numpy as jnp
from jax import lax
from jax.experimental import pallas as pl
from jax.experimental.pallas import tpu as pltpu
from jax.sharding import PartitionSpec as P

ITERS = 2
PRIOR_WEIGHT = 0.5
EPSILON = 1e-06
CONTRAST = 0.1
AMPLITUDE = math.sqrt(1.0 - CONTRAST * CONTRAST)
SIDE = 256
PIXELS = SIDE * SIDE
N_MIC, N_BIN, N_Z, N_Y = 8, 32, 8, 4
OWN, MINE = 8, 4
ROWS = 32


def hartley(side):
    k = lax.broadcasted_iota(jnp.int32, (side, side), 0)
    x = lax.broadcasted_iota(jnp.int32, (side, side), 1)
    angles = (k * x % side).astype(jnp.float32) * (2.0 * math.pi / side)
    return ((jnp.cos(angles) + jnp.sin(angles)) / math.sqrt(side)).astype(jnp.bfloat16)


def transform(images, offsets):
    basis = hartley(SIDE)
    r = lax.broadcasted_iota(jnp.int32, (MINE, SIDE, SIDE), 1)
    c = lax.broadcasted_iota(jnp.int32, (MINE, SIDE, SIDE), 2)
    take_rows = (c == (r + offsets[0][:, None, None]) % SIDE).astype(jnp.bfloat16)
    take_columns = (r == (c + offsets[1][:, None, None]) % SIDE).astype(jnp.bfloat16)
    dot = functools.partial(jnp.einsum, preferred_element_type=jnp.float32)
    moved = dot("prx,pxc->prc", take_rows, images).astype(jnp.bfloat16)
    moved = dot("prx,pxc->prc", moved, take_columns).astype(jnp.bfloat16)
    half = dot("kx,pxy->pky", basis, moved).astype(jnp.bfloat16)
    return dot("pky,ly->pkl", half, basis).astype(jnp.bfloat16)


def refine_kernel(place_ref, valid_ref, group_ref, focus_ref, damp_ref, spectra_ref, refs_ref,
                  out_ref, score_ref, ctf_ref, num_ref, den_ref, weight_ref):
    slot = lax.broadcasted_iota(jnp.int32, (N_MIC, SIDE), 0)
    focus = jnp.zeros((N_MIC, SIDE), jnp.float32)
    damp = jnp.zeros((N_MIC, SIDE), jnp.float32)
    for s in range(N_MIC):
        group = group_ref[s]
        focus = jnp.where(slot == s, focus_ref[group], focus)
        damp = jnp.where(slot == s, damp_ref[group], damp)
    k = lax.broadcasted_iota(jnp.int32, (N_MIC, SIDE), 1)
    folded = jnp.minimum(k, SIDE - k).astype(jnp.float32) / (SIDE / 2.0)
    square = folded * folded
    sine, cosine = jnp.sin(focus * square), jnp.cos(focus * square)
    envelope = jnp.exp(-damp * square)
    row_sine = jnp.transpose(-sine * envelope)
    row_cosine = jnp.transpose(-cosine * envelope)
    col_sine = (AMPLITUDE * cosine - CONTRAST * sine) * envelope
    col_cosine = (AMPLITUDE * sine + CONTRAST * cosine) * envelope
    for s in range(N_MIC):
        ctf_ref[s] = (
            row_sine[:, s : s + 1] * col_sine[s : s + 1, :]
            + row_cosine[:, s : s + 1] * col_cosine[s : s + 1, :]
        )
    out_ref[...] = refs_ref[...]
    score_ref[...] = jnp.zeros_like(score_ref)

    def chunk(i):
        return pl.ds(pl.multiple_of(i * ROWS, ROWS), ROWS)

    def one_place(p, _):
        count = jnp.int32(0)
        for s in range(N_MIC):
            count += jnp.where((place_ref[s] == p) & (valid_ref[s] > 0), 1, 0)

        @pl.when(count > 0)
        def _():
            @pl.loop(0, ITERS)
            def _(iteration):
                num_ref[...] = jnp.zeros_like(num_ref)
                den_ref[...] = jnp.zeros_like(den_ref)

                @pl.loop(0, N_MIC)
                def _(s):
                    @pl.when((place_ref[s] == p) & (valid_ref[s] > 0))
                    def _():
                        def correlate(i, sums):
                            cross, model, data = sums
                            predicted = ctf_ref[s, chunk(i), :] * out_ref[p, chunk(i), :].astype(jnp.float32)
                            values = spectra_ref[s, chunk(i), :].astype(jnp.float32)
                            return (
                                cross + predicted * values,
                                model + predicted * predicted,
                                data + values * values,
                            )

                        zero = jnp.zeros((ROWS, SIDE), jnp.float32)
                        cross, model, data = lax.fori_loop(0, SIDE // ROWS, correlate, (zero, zero, zero))
                        cross = jnp.sum(cross, keepdims=True) / PIXELS
                        model = jnp.sum(model, keepdims=True) / PIXELS + EPSILON
                        data = jnp.sum(data, keepdims=True) / PIXELS + EPSILON
                        correlation = cross / jnp.sqrt(model * data)
                        weight = 1.0 / (1.0 + jnp.exp(-SIDE * correlation))
                        weight = weight.astype(jnp.bfloat16).astype(jnp.float32)
                        score_ref[pl.ds(s, 1), :] = jnp.broadcast_to(correlation, (1, 128))

                        def gather(i, _):
                            table = ctf_ref[s, chunk(i), :]
                            scaled = weight * table
                            values = spectra_ref[s, chunk(i), :].astype(jnp.float32)
                            term = (scaled * values).astype(jnp.bfloat16).astype(jnp.float32)
                            num_ref[chunk(i), :] += term
                            den_ref[chunk(i), :] += scaled * table
                            return 0

                        lax.fori_loop(0, SIDE // ROWS, gather, 0)

                def update(i, _):
                    previous = out_ref[p, chunk(i), :].astype(jnp.float32)
                    top = num_ref[chunk(i), :] + PRIOR_WEIGHT * previous
                    out_ref[p, chunk(i), :] = (top / (den_ref[chunk(i), :] + PRIOR_WEIGHT)).astype(jnp.bfloat16)
                    return 0

                lax.fori_loop(0, SIDE // ROWS, update, 0)

        return 0

    lax.fori_loop(0, OWN, one_place, 0)


def refine(place, valid, group, defocus, bfactor, spectra, references):
    smem = pl.BlockSpec(memory_space=pltpu.SMEM)
    vmem = pl.BlockSpec(memory_space=pltpu.VMEM)
    return pl.pallas_call(
        refine_kernel,
        out_shape=(
            jax.ShapeDtypeStruct((OWN, SIDE, SIDE), jnp.bfloat16),
            jax.ShapeDtypeStruct((N_MIC, 128), jnp.float32),
        ),
        in_specs=[smem] * 5 + [vmem] * 2,
        out_specs=(vmem, vmem),
        scratch_shapes=[
            pltpu.VMEM((N_MIC, SIDE, SIDE), jnp.float32),
            pltpu.VMEM((SIDE, SIDE), jnp.float32),
            pltpu.VMEM((SIDE, SIDE), jnp.float32),
            pltpu.VMEM((N_MIC, 128), jnp.float32),
        ],
        compiler_params=pltpu.CompilerParams(vmem_limit_bytes=24 << 20),
        name="refine",
    )(place, valid, group, defocus, bfactor, spectra, references)


def pick_kernel(index_ref, tile_ref, out_ref):
    out_ref[...] = tile_ref[...]


def pick(tiles, index):
    return pl.pallas_call(
        pick_kernel,
        out_shape=jax.ShapeDtypeStruct((index.shape[0], SIDE, SIDE), tiles.dtype),
        grid_spec=pltpu.PrefetchScalarGridSpec(
            num_scalar_prefetch=1,
            grid=(index.shape[0],),
            in_specs=[pl.BlockSpec((1, SIDE, SIDE), lambda i, index: (index[i], 0, 0))],
            out_specs=pl.BlockSpec((1, SIDE, SIDE), lambda i, index: (i, 0, 0)),
        ),
        name="pick",
    )(index, tiles)


def body(images, offsets, ctf_group, particle_bin, bin_place, defocus, bfactor, references):
    mic, column = lax.axis_index("mic"), lax.axis_index("bin")
    my_y, my_z = column % N_Y, column // N_Y
    places = jnp.take(bin_place, particle_bin)
    labels = lax.all_gather(jnp.stack([places, ctf_group]), ("mic", "bin"))
    place_of = labels[:, 0].reshape(N_MIC, N_BIN * MINE)
    group_of = labels[:, 1].reshape(N_MIC, N_BIN * MINE)
    spectra = transform(images, offsets)

    lines = [[z * N_Y + y for z in range(N_Z)] for y in range(N_Y)]
    line = lax.all_gather(spectra, "bin", axis_index_groups=lines).reshape(N_Z * MINE, SIDE, SIDE)
    row = jnp.take(place_of, mic, axis=0).reshape(N_Z, N_Y, MINE)
    owner = row // OWN
    to_mic, to_z, to_y = owner // N_BIN, owner % N_BIN // N_Y, owner % N_Y
    line_z = jnp.take(to_z, my_y, axis=1).reshape(N_Z * MINE)
    line_y = jnp.take(to_y, my_y, axis=1).reshape(N_Z * MINE)
    order = jnp.arange(N_Z * MINE)
    for_y = (line_z == my_z)[None, :] & (line_y[None, :] == jnp.arange(N_Y)[:, None])
    rank = jnp.sum(for_y[:, None, :] & (order[None, :] < order[:, None])[None], axis=2)
    first = for_y[:, None, :] & (rank[:, None, :] == jnp.arange(MINE)[None, :, None])
    first = jnp.sum(first * order, axis=2)
    packed = pick(line, first.reshape(N_Y * MINE)).reshape(N_Y, MINE, SIDE, SIDE)
    planes = [[z * N_Y + y for y in range(N_Y)] for z in range(N_Z)]
    plane = lax.all_to_all(packed, "bin", 0, 0, axis_index_groups=planes, tiled=True)
    plane = plane.reshape(N_Y * MINE, SIDE, SIDE)
    here = (to_z == my_z) & (to_y == my_y)
    here_line = jnp.transpose(here, (1, 0, 2)).reshape(N_Y, N_Z * MINE)
    mic_line = jnp.transpose(to_mic, (1, 0, 2)).reshape(N_Y, N_Z * MINE)
    rank = jnp.sum(here_line[:, None, :] & (order[None, :] < order[:, None])[None], axis=2)
    position = jnp.arange(N_Y)[:, None] * MINE + rank
    chosen = here_line[None] & (mic_line[None] == jnp.arange(N_MIC)[:, None, None])
    second = jnp.sum(chosen * position[None], axis=(1, 2))
    sent = pick(plane, second)
    owned = lax.all_to_all(sent, "mic", 0, 0, tiled=True)

    mine = place_of // OWN == mic * N_BIN + column
    valid = jnp.sum(mine, axis=1).astype(jnp.int32)
    place = jnp.sum(mine * (place_of % OWN), axis=1)
    group = jnp.sum(mine * group_of, axis=1)
    refined, correlations = refine(place, valid, group, defocus, bfactor, owned, references)
    every = lax.all_gather(correlations[:, 0], ("mic", "bin"))
    scores = jnp.take(every.reshape(-1), places // OWN * N_MIC + mic)
    return (refined, scores)


def solution(mesh):
    tiles, items = P(("mic", "bin"), None, None), P(("mic", "bin"))
    return jax.shard_map(
        body,
        mesh=mesh,
        in_specs=(tiles, P(None, ("mic", "bin")), items, items, P(), P(), P(), tiles),
        out_specs=(tiles, items),
        check_vma=False,
    )
```

```python
import functools
import math

import jax
import jax.numpy as jnp
from jax import lax
from jax.experimental import pallas as pl
from jax.experimental.pallas import tpu as pltpu
from jax.sharding import PartitionSpec as P

ITERS = 2
PRIOR_WEIGHT = 0.5
EPSILON = 1e-06
CONTRAST = 0.1
AMPLITUDE = math.sqrt(1.0 - CONTRAST * CONTRAST)
SIDE = 256
PIXELS = SIDE * SIDE
N_MIC, N_BIN, N_Z, N_Y = 8, 32, 8, 4
OWN, MINE = 8, 4
ROWS = 32
CTF_GROUPS = 64
CHUNKS = 4
DEPTH = SIDE // CHUNKS
MESH = pl.DeviceIdType.MESH


def hartley(side):
    k = lax.broadcasted_iota(jnp.int32, (side, side), 0)
    x = lax.broadcasted_iota(jnp.int32, (side, side), 1)
    angles = (k * x % side).astype(jnp.float32) * (2.0 * math.pi / side)
    return ((jnp.cos(angles) + jnp.sin(angles)) / math.sqrt(side)).astype(jnp.bfloat16)


def transform(images, offsets):
    basis = hartley(SIDE)
    r = lax.broadcasted_iota(jnp.int32, (MINE, SIDE, SIDE), 1)
    c = lax.broadcasted_iota(jnp.int32, (MINE, SIDE, SIDE), 2)
    take_rows = (c == (r + offsets[0][:, None, None]) % SIDE).astype(jnp.bfloat16)
    take_columns = (r == (c + offsets[1][:, None, None]) % SIDE).astype(jnp.bfloat16)
    dot = functools.partial(jnp.einsum, preferred_element_type=jnp.float32)
    moved = dot("prx,pxc->prc", take_rows, images).astype(jnp.bfloat16)
    moved = dot("prx,pxc->prc", moved, take_columns).astype(jnp.bfloat16)
    half = dot("kx,pxy->pky", basis, moved).astype(jnp.bfloat16)
    return dot("pky,ly->pkl", half, basis).astype(jnp.bfloat16)


def refine_kernel(label_ref, focus_ref, damp_ref, spectra_ref, refs_ref,
                  out_ref, score_ref, ctf_ref, num_ref, den_ref):
    slot = lax.broadcasted_iota(jnp.int32, (N_MIC, SIDE), 0)
    focus = jnp.zeros((N_MIC, SIDE), jnp.float32)
    damp = jnp.zeros((N_MIC, SIDE), jnp.float32)
    for s in range(N_MIC):
        group = (label_ref[s, 0] - 1) & (CTF_GROUPS - 1)
        focus = jnp.where(slot == s, focus_ref[group], focus)
        damp = jnp.where(slot == s, damp_ref[group], damp)
    k = lax.broadcasted_iota(jnp.int32, (N_MIC, SIDE), 1)
    folded = jnp.minimum(k, SIDE - k).astype(jnp.float32) / (SIDE / 2.0)
    square = folded * folded
    sine, cosine = jnp.sin(focus * square), jnp.cos(focus * square)
    envelope = jnp.exp(-damp * square)
    row_sine = jnp.transpose(-sine * envelope)
    row_cosine = jnp.transpose(-cosine * envelope)
    col_sine = (AMPLITUDE * cosine - CONTRAST * sine) * envelope
    col_cosine = (AMPLITUDE * sine + CONTRAST * cosine) * envelope
    for s in range(N_MIC):
        ctf_ref[s] = (
            row_sine[:, s : s + 1] * col_sine[s : s + 1, :]
            + row_cosine[:, s : s + 1] * col_cosine[s : s + 1, :]
        )
    out_ref[...] = refs_ref[...]
    score_ref[...] = jnp.zeros_like(score_ref)

    def chunk(i):
        return pl.ds(pl.multiple_of(i * ROWS, ROWS), ROWS)

    def kept_at(s, p):
        code = label_ref[s, 0]
        return (code > 0) & ((((code - 1) >> 6) & (OWN - 1)) == p)

    def one_place(p, _):
        count = jnp.int32(0)
        for s in range(N_MIC):
            count += jnp.where(kept_at(s, p), 1, 0)

        @pl.when(count > 0)
        def _():
            @pl.loop(0, ITERS)
            def _(iteration):
                num_ref[...] = jnp.zeros_like(num_ref)
                den_ref[...] = jnp.zeros_like(den_ref)

                @pl.loop(0, N_MIC)
                def _(s):
                    @pl.when(kept_at(s, p))
                    def _():
                        def correlate(i, sums):
                            cross, model, data = sums
                            predicted = ctf_ref[s, chunk(i), :] * out_ref[p, chunk(i), :].astype(jnp.float32)
                            values = spectra_ref[s, chunk(i), :].astype(jnp.float32)
                            return (
                                cross + predicted * values,
                                model + predicted * predicted,
                                data + values * values,
                            )

                        zero = jnp.zeros((ROWS, SIDE), jnp.float32)
                        cross, model, data = lax.fori_loop(0, SIDE // ROWS, correlate, (zero, zero, zero))
                        cross = jnp.sum(cross, keepdims=True) / PIXELS
                        model = jnp.sum(model, keepdims=True) / PIXELS + EPSILON
                        data = jnp.sum(data, keepdims=True) / PIXELS + EPSILON
                        correlation = cross / jnp.sqrt(model * data)
                        weight = 1.0 / (1.0 + jnp.exp(-SIDE * correlation))
                        weight = weight.astype(jnp.bfloat16).astype(jnp.float32)
                        score_ref[s] = jnp.broadcast_to(correlation, (8, 128))

                        def gather(i, _):
                            table = ctf_ref[s, chunk(i), :]
                            scaled = weight * table
                            values = spectra_ref[s, chunk(i), :].astype(jnp.float32)
                            term = (scaled * values).astype(jnp.bfloat16).astype(jnp.float32)
                            num_ref[chunk(i), :] += term
                            den_ref[chunk(i), :] += scaled * table
                            return 0

                        lax.fori_loop(0, SIDE // ROWS, gather, 0)

                def update(i, _):
                    previous = out_ref[p, chunk(i), :].astype(jnp.float32)
                    top = num_ref[chunk(i), :] + PRIOR_WEIGHT * previous
                    out_ref[p, chunk(i), :] = (top / (den_ref[chunk(i), :] + PRIOR_WEIGHT)).astype(jnp.bfloat16)
                    return 0

                lax.fori_loop(0, SIDE // ROWS, update, 0)

        return 0

    lax.fori_loop(0, OWN, one_place, 0)


def refine(labels, defocus, bfactor, spectra, references):
    smem = pl.BlockSpec(memory_space=pltpu.SMEM)
    vmem = pl.BlockSpec(memory_space=pltpu.VMEM)
    return pl.pallas_call(
        refine_kernel,
        out_shape=(
            jax.ShapeDtypeStruct((OWN, SIDE, SIDE), jnp.bfloat16),
            jax.ShapeDtypeStruct((N_MIC, 8, 128), jnp.float32),
        ),
        in_specs=[smem] * 3 + [vmem] * 2,
        out_specs=(vmem, vmem),
        scratch_shapes=[
            pltpu.VMEM((N_MIC, SIDE, SIDE), jnp.float32),
            pltpu.VMEM((SIDE, SIDE), jnp.float32),
            pltpu.VMEM((SIDE, SIDE), jnp.float32),
        ],
        compiler_params=pltpu.CompilerParams(vmem_limit_bytes=24 << 20),
        name="refine",
    )(labels, defocus, bfactor, spectra, references)


def code_of(bin_ref, place_ref, group_ref, j):
    return place_ref[bin_ref[j]] * CTF_GROUPS + group_ref[j] + 1


def meet(peers):
    barrier = pltpu.get_barrier_semaphore()
    for peer in peers:
        pl.semaphore_signal(barrier, inc=1, device_id=peer, device_id_type=MESH)
    pl.semaphore_wait(barrier, len(peers))


def lanes_of(values):
    lane = lax.broadcasted_iota(jnp.int32, (8, 128), 1)
    tile = jnp.zeros((8, 128), jnp.int32)
    for j, value in enumerate(values):
        tile = jnp.where(lane == j, value, tile)
    return tile


def route_kernel(bin_ref, bin_place_ref, group_ref, spectra_ref, out_ref, label_ref, *scratch):
    lines, packs = scratch[:CHUNKS], scratch[CHUNKS : 2 * CHUNKS]
    planes, parcels = scratch[2 * CHUNKS : 3 * CHUNKS], scratch[3 * CHUNKS : 4 * CHUNKS]
    (line_label, pack_label, plane_label, parcel_label, mine_label, line_code, plane_code,
     z_send, z_recv, y_send, y_recv, m_send, m_recv, zl_send, zl_recv, yl_send, yl_recv,
     ml_send, ml_recv, code_sem) = scratch[4 * CHUNKS :]
    mic, column = lax.axis_index("mic"), lax.axis_index("bin")
    z, y = column // N_Y, lax.rem(column, N_Y)

    def at_z(d):
        return (mic, lax.rem(z + d, N_Z) * N_Y + y)

    def at_y(d):
        return (mic, z * N_Y + lax.rem(y + d, N_Y))

    def at_mic(d):
        return (lax.rem(mic + d, N_MIC), column)

    def send(src, dst, send_sem, recv_sem, peer):
        copy = pltpu.make_async_remote_copy(
            src_ref=src, dst_ref=dst, send_sem=send_sem, recv_sem=recv_sem,
            device_id=peer, device_id_type=MESH,
        )
        copy.start()
        copies.append(copy)
        return copy

    copies = []
    meet([at_z(d) for d in range(1, N_Z)] + [at_y(d) for d in range(1, N_Y)] + [at_mic(d) for d in range(1, N_MIC)])

    line_label[0] = lanes_of([code_of(bin_ref, bin_place_ref, group_ref, j) for j in range(MINE)])
    line_labels = [
        send(line_label.at[0], line_label.at[N_Z - d], zl_send.at[d - 1], zl_recv.at[d - 1], at_z(d))
        for d in range(1, N_Z)
    ]
    hops, y_copies, m_copies = {}, {}, {}
    pick_line, pick_plane = [], []
    half = N_Z // 2

    def hop(c, h):
        line = lines[c]
        if h == 1:
            line[0:MINE] = spectra_ref[:, c * DEPTH : (c + 1) * DEPTH, :]
        for way in range(2):
            if h > 1:
                hops[c, way, h - 1].wait_recv()
            src = lax_mod(1 - h, N_Z) if way == 0 else h - 1
            dst = N_Z - h if way == 0 else h
            low, count = 0, MINE
            if h == half:
                low, count = (MINE // 2) * way, MINE // 2
            hops[c, way, h] = send(
                line.at[pl.ds(src * MINE + low, count)], line.at[pl.ds(dst * MINE + low, count)],
                z_send.at[c, way, h - 1], z_recv.at[c, way, h - 1], at_z(1 if way == 0 else N_Z - 1),
            )

    def choose_line():
        for copy in line_labels:
            copy.wait_recv()
        fetch = pltpu.make_async_copy(line_label, line_code, code_sem.at[0])
        fetch.start()
        fetch.wait()
        keys = [[jnp.int32(0)] * MINE for _ in range(N_Y)]
        counts = [jnp.int32(0)] * N_Y
        for t in range(N_Z * MINE):
            code = line_code[t // MINE, 0, t % MINE]
            owner = (code - 1) >> 9
            here = ((owner >> 2) & (N_Z - 1)) == z
            away = (owner - y) & (N_Y - 1)
            key = code * (N_Z * MINE) + t
            for d in range(N_Y):
                hit = here & (away == d)
                rank = jnp.where(hit, counts[d], MINE)
                counts[d] = counts[d] + jnp.where(hit, 1, 0)
                keys[d] = [jnp.where(rank == k, key, keys[d][k]) for k in range(MINE)]
        pick_line.extend([[key & (N_Z * MINE - 1) for key in keys[d]] for d in range(N_Y)])
        for d in range(N_Y):
            tile = lanes_of([key >> 5 for key in keys[d]])
            if d == 0:
                plane_label[0] = tile
            else:
                pack_label[d - 1] = tile

    def to_plane(c):
        for way in range(2):
            hops[c, way, half].wait_recv()
        for d in range(N_Y):
            for k in range(MINE):
                tile = lines[c][pick_line[d][k]]
                if d == 0:
                    planes[c][k] = tile
                else:
                    packs[c][(d - 1) * MINE + k] = tile
        for d in range(1, N_Y):
            y_copies[c, d] = send(
                packs[c].at[pl.ds((d - 1) * MINE, MINE)], planes[c].at[pl.ds((N_Y - d) * MINE, MINE)],
                y_send.at[c, d - 1], y_recv.at[c, d - 1], at_y(d),
            )

    def choose_plane():
        fetch = pltpu.make_async_copy(plane_label, plane_code, code_sem.at[1])
        fetch.start()
        fetch.wait()
        keys = [jnp.int32(0)] * N_MIC
        for s in range(N_Y * MINE):
            code = plane_code[s // MINE, 0, s % MINE]
            away = (((code - 1) >> 14) - mic) & (N_MIC - 1)
            away = jnp.where(code > 0, away, N_MIC)
            key = code * (N_Y * MINE) + s
            keys = [jnp.where(away == d, key, keys[d]) for d in range(N_MIC)]
        pick_plane.extend([key & (N_Y * MINE - 1) for key in keys])
        for d in range(N_MIC):
            tile = jnp.full((8, 128), keys[d] >> 4, jnp.int32)
            if d == 0:
                mine_label[0] = tile
            else:
                parcel_label[d - 1] = tile

    def to_owner(c):
        for d in range(1, N_Y):
            y_copies[c, d].wait_recv()
        rows = pl.ds(c * DEPTH, DEPTH)
        for d in range(N_MIC):
            tile = planes[c][pick_plane[d]]
            if d == 0:
                out_ref[0, rows, :] = tile
            else:
                parcels[c][d - 1] = tile
        for d in range(1, N_MIC):
            m_copies[c, d] = send(
                parcels[c].at[d - 1], out_ref.at[N_MIC - d, rows, :],
                m_send.at[c, d - 1], m_recv.at[c, d - 1], at_mic(d),
            )

    plane_labels, mine_labels = [], []
    for step in range(1, 2 * CHUNKS + half + 3):
        for c in range(CHUNKS):
            h = step - 2 * c
            if 1 <= h <= half:
                hop(c, h)
            elif h == half + 1:
                if c == 0:
                    choose_line()
                    plane_labels += [
                        send(pack_label.at[d - 1], plane_label.at[N_Y - d], yl_send.at[d - 1], yl_recv.at[d - 1], at_y(d))
                        for d in range(1, N_Y)
                    ]
                to_plane(c)
            elif h == half + 3:
                if c == 0:
                    for copy in plane_labels:
                        copy.wait_recv()
                    choose_plane()
                    mine_labels += [
                        send(parcel_label.at[d - 1], mine_label.at[N_MIC - d], ml_send.at[d - 1], ml_recv.at[d - 1], at_mic(d))
                        for d in range(1, N_MIC)
                    ]
                to_owner(c)
    for copy in mine_labels:
        copy.wait_recv()
    for d in range(N_MIC):
        label_ref[pl.ds(d, 1), :] = mine_label[d, 0:1, :]
    for copy in m_copies.values():
        copy.wait_recv()
    for copy in copies:
        copy.wait_send()


def lax_mod(a, n):
    return a % n


def route(particle_bin, bin_place, ctf_group, spectra):
    smem = pl.BlockSpec(memory_space=pltpu.SMEM)
    vmem = pl.BlockSpec(memory_space=pltpu.VMEM)
    buffers = [pltpu.VMEM((n, DEPTH, SIDE), jnp.bfloat16)
               for n in (N_Z * MINE, (N_Y - 1) * MINE, N_Y * MINE, N_MIC - 1) for _ in range(CHUNKS)]
    labels = [pltpu.VMEM((n, 8, 128), jnp.int32) for n in (N_Z, N_Y - 1, N_Y, N_MIC - 1, N_MIC)]
    codes = [pltpu.SMEM((n, 8, 128), jnp.int32) for n in (N_Z, N_Y)]
    dma = pltpu.SemaphoreType.DMA
    sems = [dma(shape) for shape in ((CHUNKS, 2, N_Z // 2), (CHUNKS, N_Y - 1), (CHUNKS, N_MIC - 1),
                                     (N_Z - 1,), (N_Y - 1,), (N_MIC - 1,)) for _ in range(2)]
    return pl.pallas_call(
        route_kernel,
        out_shape=(
            jax.ShapeDtypeStruct((N_MIC, SIDE, SIDE), jnp.bfloat16),
            jax.ShapeDtypeStruct((N_MIC, 128), jnp.int32),
        ),
        in_specs=[smem] * 3 + [vmem],
        out_specs=(vmem, vmem),
        scratch_shapes=buffers + labels + codes + sems + [dma((2,))],
        compiler_params=pltpu.CompilerParams(
            collective_id=0, has_side_effects=True, vmem_limit_bytes=24 << 20
        ),
        name="route",
    )(particle_bin, bin_place, ctf_group, spectra)


def answer_kernel(bin_ref, bin_place_ref, score_ref, out_ref, row, column_scores, m_send, m_recv, b_send, b_recv):
    mic, column = lax.axis_index("mic"), lax.axis_index("bin")
    at_mic = [(lax.rem(mic + d, N_MIC), column) for d in range(N_MIC)]
    at_bin = [(mic, lax.rem(column + d, N_BIN)) for d in range(N_BIN)]
    meet(at_mic[1:] + at_bin[1:])
    copies = []
    for d in range(1, N_MIC):
        copies.append(pltpu.make_async_remote_copy(
            src_ref=score_ref.at[d], dst_ref=row.at[N_MIC - d], send_sem=m_send.at[d - 1],
            recv_sem=m_recv.at[d - 1], device_id=at_mic[d], device_id_type=MESH))
        copies[-1].start()
    row[0] = score_ref[0]
    for copy in copies:
        copy.wait_recv()
    for d in range(N_MIC):
        column_scores[0, pl.ds(d, 1), :] = row[d, 0:1, :]
    spread = []
    for d in range(1, N_BIN):
        spread.append(pltpu.make_async_remote_copy(
            src_ref=column_scores.at[0], dst_ref=column_scores.at[N_BIN - d], send_sem=b_send.at[d - 1],
            recv_sem=b_recv.at[d - 1], device_id=at_bin[d], device_id_type=MESH))
        spread[-1].start()
    for copy in spread:
        copy.wait_recv()
    lane = lax.broadcasted_iota(jnp.int32, (8, 128), 1)
    scores = jnp.zeros((8, 128), jnp.float32)
    for j in range(MINE):
        owner = bin_place_ref[bin_ref[j]] // OWN
        r = (owner - column) & (N_BIN - 1)
        q = ((owner >> 5) - mic) & (N_MIC - 1)
        scores = jnp.where(lane == j, column_scores[r, pl.ds(q, 1), :], scores)
    out_ref[...] = scores
    for copy in copies + spread:
        copy.wait_send()


def answer(particle_bin, bin_place, correlations):
    smem = pl.BlockSpec(memory_space=pltpu.SMEM)
    vmem = pl.BlockSpec(memory_space=pltpu.VMEM)
    dma = pltpu.SemaphoreType.DMA
    return pl.pallas_call(
        answer_kernel,
        out_shape=jax.ShapeDtypeStruct((8, 128), jnp.float32),
        in_specs=[smem, smem, vmem],
        out_specs=vmem,
        scratch_shapes=[
            pltpu.VMEM((N_MIC, 8, 128), jnp.float32),
            pltpu.VMEM((N_BIN, 8, 128), jnp.float32),
            dma((N_MIC - 1,)), dma((N_MIC - 1,)), dma((N_BIN - 1,)), dma((N_BIN - 1,)),
        ],
        compiler_params=pltpu.CompilerParams(collective_id=1, has_side_effects=True),
        name="answer",
    )(particle_bin, bin_place, correlations)


def body(images, offsets, ctf_group, particle_bin, bin_place, defocus, bfactor, references):
    spectra = transform(images, offsets)
    owned, labels = route(particle_bin, bin_place, ctf_group, spectra)
    refined, correlations = refine(labels, defocus, bfactor, owned, references)
    scores = answer(particle_bin, bin_place, correlations)
    return (refined, scores[0, :MINE])


def solution(mesh):
    tiles, items = P(("mic", "bin"), None, None), P(("mic", "bin"))
    return jax.shard_map(
        body,
        mesh=mesh,
        in_specs=(tiles, P(None, ("mic", "bin")), items, items, P(), P(), P(), tiles),
        out_specs=(tiles, items),
        check_vma=False,
    )
```

```python
import math

import jax
import jax.numpy as jnp
from jax import lax
from jax.experimental import pallas as pl
from jax.experimental.pallas import tpu as pltpu
from jax.sharding import PartitionSpec as P

PRIOR_WEIGHT = 0.5
EPSILON = 1e-06
CONTRAST = 0.1
AMPLITUDE = math.sqrt(1.0 - CONTRAST * CONTRAST)
SIDE = 256
PIXELS = SIDE * SIDE
N_MIC, N_BIN, N_Z, N_Y = 8, 32, 8, 4
OWN, MINE = 8, 4
ROWS = 32
CTF_GROUPS = 64
DEPTHS = (64, 64, 64, 64)
CHUNKS = len(DEPTHS)
STARTS = [sum(DEPTHS[:c]) for c in range(CHUNKS)]
LAG = 2
MESH = pl.DeviceIdType.MESH


def hartley(side):
    k = lax.broadcasted_iota(jnp.int32, (side, side), 0)
    x = lax.broadcasted_iota(jnp.int32, (side, side), 1)
    angles = (k * x % side).astype(jnp.float32) * (2.0 * math.pi / side)
    return ((jnp.cos(angles) + jnp.sin(angles)) / math.sqrt(side)).astype(jnp.bfloat16)


def code_of(bin_ref, place_ref, group_ref, j):
    return place_ref[bin_ref[j]] * CTF_GROUPS + group_ref[j] + 1


def lanes_of(values):
    lane = lax.broadcasted_iota(jnp.int32, (8, 128), 1)
    tile = jnp.zeros((8, 128), jnp.int32)
    for j, value in enumerate(values):
        tile = jnp.where(lane == j, value, tile)
    return tile


def transform(offset_ref, basis_ref, images_ref, spectra):
    r = lax.broadcasted_iota(jnp.int32, (SIDE, SIDE), 0)
    c = lax.broadcasted_iota(jnp.int32, (SIDE, SIDE), 1)

    def one_hot(mask):
        return jnp.where(mask, 1.0, 0.0).astype(jnp.bfloat16)

    def dot(a, b):
        return jnp.dot(a, b, preferred_element_type=jnp.float32).astype(jnp.bfloat16)

    for j in range(MINE):
        moved = dot(one_hot(c == ((r + offset_ref[0, j]) & (SIDE - 1))), images_ref[j])
        moved = dot(moved, one_hot(r == ((c + offset_ref[1, j]) & (SIDE - 1))))
        spectra[j] = dot(dot(basis_ref[...], moved), basis_ref[...])


def kernel(bin_ref, bin_place_ref, group_ref, offset_ref, focus_ref, damp_ref, basis_ref, images_ref, refs_ref,
           out_ref, score_ref, *scratch):
    lines, packs = scratch[:CHUNKS], scratch[CHUNKS : 2 * CHUNKS]
    planes, parcels = scratch[2 * CHUNKS : 3 * CHUNKS], scratch[3 * CHUNKS : 4 * CHUNKS]
    (line_label, pack_label, plane_label, parcel_label, mine_label, line_code, plane_code, mine_code,
     z_send, z_recv, y_send, y_recv, m_send, m_recv, zl_send, zl_recv, yl_send, yl_recv,
     ml_send, ml_recv, am_send, am_recv, ay_send, ay_recv, az_send, az_recv, code_sem,
     spectra, owned, ctf, sums, total, row_scores, row, plane_scores, line_scores) = scratch[4 * CHUNKS :]
    mic, column = lax.axis_index("mic"), lax.axis_index("bin")
    z, y = column >> 2, column & (N_Y - 1)

    def at_z(d):
        return (mic, (((z + d) & (N_Z - 1)) << 2) + y)

    def at_y(d):
        return (mic, (z << 2) + ((y + d) & (N_Y - 1)))

    def at_mic(d):
        return ((mic + d) & (N_MIC - 1), column)

    def send(src, dst, send_sem, recv_sem, peer):
        copy = pltpu.make_async_remote_copy(
            src_ref=src, dst_ref=dst, send_sem=send_sem, recv_sem=recv_sem,
            device_id=peer, device_id_type=MESH,
        )
        copy.start()
        copies.append(copy)
        return copy

    copies = []
    peers = [at_z(d) for d in range(1, N_Z)] + [at_y(d) for d in range(1, N_Y)] + [at_mic(d) for d in range(1, N_MIC)]
    barrier = pltpu.get_barrier_semaphore()
    for peer in peers:
        pl.semaphore_signal(barrier, inc=1, device_id=peer, device_id_type=MESH)
    transform(offset_ref, basis_ref, images_ref, spectra)
    for block in range(2):
        total[block, N_MIC] = jnp.zeros((ROWS, SIDE), jnp.float32)
    sums[...] = jnp.zeros_like(sums)
    pl.semaphore_wait(barrier, len(peers))


    hops, y_copies, m_copies = {}, {}, {}
    pick_line, pick_plane = [], []
    half = N_Z // 2

    def hop(c, h):
        line = lines[c]
        if h == 1:
            line[0:MINE] = spectra[:, STARTS[c] : STARTS[c] + DEPTHS[c], :]
        for way in range(2):
            if h > 1:
                hops[c, way, h - 1].wait_recv()
            src = (1 - h) % N_Z if way == 0 else h - 1
            dst = N_Z - h if way == 0 else h
            low, count = 0, MINE
            if h == half:
                low, count = (MINE // 2) * way, MINE // 2
            hops[c, way, h] = send(
                line.at[pl.ds(src * MINE + low, count)], line.at[pl.ds(dst * MINE + low, count)],
                z_send.at[c, way, h - 1], z_recv.at[c, way, h - 1], at_z(1 if way == 0 else N_Z - 1),
            )

    def choose_line():
        for copy in line_labels:
            copy.wait_recv()
        fetch = pltpu.make_async_copy(line_label, line_code, code_sem.at[0])
        fetch.start()
        fetch.wait()
        keys = [[jnp.int32(0)] * MINE for _ in range(N_Y)]
        counts = [jnp.int32(0)] * N_Y
        for t in range(N_Z * MINE):
            code = line_code[t // MINE, 0, t % MINE]
            owner = (code - 1) >> 9
            here = ((owner >> 2) & (N_Z - 1)) == z
            away = (owner - y) & (N_Y - 1)
            key = code * (N_Z * MINE) + t
            for d in range(N_Y):
                hit = here & (away == d)
                rank = jnp.where(hit, counts[d], MINE)
                counts[d] = counts[d] + jnp.where(hit, 1, 0)
                keys[d] = [jnp.where(rank == k, key, keys[d][k]) for k in range(MINE)]
        pick_line.extend([[key & (N_Z * MINE - 1) for key in keys[d]] for d in range(N_Y)])
        for d in range(N_Y):
            tile = lanes_of([key >> 5 for key in keys[d]])
            if d == 0:
                plane_label[0] = tile
            else:
                pack_label[d - 1] = tile

    def to_plane(c):
        for way in range(2):
            hops[c, way, half].wait_recv()
        for d in range(N_Y):
            for k in range(MINE):
                tile = lines[c][pick_line[d][k]]
                if d == 0:
                    planes[c][k] = tile
                else:
                    packs[c][(d - 1) * MINE + k] = tile
        for d in range(1, N_Y):
            y_copies[c, d] = send(
                packs[c].at[pl.ds((d - 1) * MINE, MINE)], planes[c].at[pl.ds((N_Y - d) * MINE, MINE)],
                y_send.at[c, d - 1], y_recv.at[c, d - 1], at_y(d),
            )

    def choose_plane():
        fetch = pltpu.make_async_copy(plane_label, plane_code, code_sem.at[1])
        fetch.start()
        fetch.wait()
        keys = [jnp.int32(0)] * N_MIC
        for s in range(N_Y * MINE):
            code = plane_code[s // MINE, 0, s % MINE]
            away = (((code - 1) >> 14) - mic) & (N_MIC - 1)
            away = jnp.where(code > 0, away, N_MIC)
            key = code * (N_Y * MINE) + s
            keys = [jnp.where(away == d, key, keys[d]) for d in range(N_MIC)]
        pick_plane.extend([key & (N_Y * MINE - 1) for key in keys])
        for d in range(N_MIC):
            tile = jnp.full((8, 128), keys[d] >> 4, jnp.int32)
            if d == 0:
                mine_label[0] = tile
            else:
                parcel_label[d - 1] = tile

    def to_owner(c):
        for d in range(1, N_Y):
            y_copies[c, d].wait_recv()
        rows = pl.ds(STARTS[c], DEPTHS[c])
        for d in range(N_MIC):
            tile = planes[c][pick_plane[d]]
            if d == 0:
                owned[0, rows, :] = tile
            else:
                parcels[c][d - 1] = tile
        for d in range(1, N_MIC):
            m_copies[c, d] = send(
                parcels[c].at[d - 1], owned.at[N_MIC - d, rows, :],
                m_send.at[c, d - 1], m_recv.at[c, d - 1], at_mic(d),
            )

    line_label[0] = lanes_of([code_of(bin_ref, bin_place_ref, group_ref, j) for j in range(MINE)])
    line_labels = [
        send(line_label.at[0], line_label.at[N_Z - d], zl_send.at[d - 1], zl_recv.at[d - 1], at_z(d))
        for d in range(1, N_Z)
    ]
    def place_of(s):
        return ((mine_code[s, 0, 0] - 1) >> 6) & (OWN - 1)

    def tables():
        for copy in mine_labels:
            copy.wait_recv()
        fetch = pltpu.make_async_copy(mine_label, mine_code, code_sem.at[2])
        fetch.start()
        fetch.wait()
        slot = lax.broadcasted_iota(jnp.int32, (N_MIC, SIDE), 0)
        focus = jnp.zeros((N_MIC, SIDE), jnp.float32)
        damp = jnp.zeros((N_MIC, SIDE), jnp.float32)
        for s in range(N_MIC):
            group = (mine_code[s, 0, 0] - 1) & (CTF_GROUPS - 1)
            focus = jnp.where(slot == s, focus_ref[group], focus)
            damp = jnp.where(slot == s, damp_ref[group], damp)
        k = lax.broadcasted_iota(jnp.int32, (N_MIC, SIDE), 1)
        folded = jnp.minimum(k, SIDE - k).astype(jnp.float32) * (2.0 / SIDE)
        square = folded * folded
        sine, cosine = jnp.sin(focus * square), jnp.cos(focus * square)
        envelope = jnp.exp(-damp * square)
        row_sine = jnp.transpose(-sine * envelope)
        row_cosine = jnp.transpose(-cosine * envelope)
        col_sine = (AMPLITUDE * cosine - CONTRAST * sine) * envelope
        col_cosine = (AMPLITUDE * sine + CONTRAST * cosine) * envelope
        for s in range(N_MIC):
            ctf[s] = (
                row_sine[:, s : s + 1] * col_sine[s : s + 1, :]
                + row_cosine[:, s : s + 1] * col_cosine[s : s + 1, :]
            )

    def collect(start, depth, source, with_data):
        @pl.loop(0, N_MIC)
        def _(s):
            place = place_of(s)
            parts = [jnp.zeros((16, SIDE), jnp.float32)] * 3
            for low in range(start, start + depth, 16):
                rows = pl.ds(low, 16)
                predicted = ctf[s, rows, :] * source[place, rows, :].astype(jnp.float32)
                values = owned[s, rows, :].astype(jnp.float32)
                parts[0] = parts[0] + predicted * values
                parts[1] = parts[1] + predicted * predicted
                if with_data:
                    parts[2] = parts[2] + values * values
            for n in range(3 if with_data else 2):
                sums[s, n] += parts[n][:8] + parts[n][8:]

    def correlate():
        slot = lax.broadcasted_iota(jnp.int32, (N_MIC, 128), 0)
        means = []
        for n in range(3):
            mean = jnp.zeros((N_MIC, 128), jnp.float32)
            for s in range(N_MIC):
                mean = jnp.where(slot == s, jnp.sum(sums[s, n], keepdims=True), mean)
            means.append(mean / PIXELS)
        correlation = means[0] / jnp.sqrt((means[1] + EPSILON) * (means[2] + EPSILON))
        weight = 1.0 / (1.0 + jnp.exp(-SIDE * correlation))
        weight = weight.astype(jnp.bfloat16).astype(jnp.float32)
        weights = [jnp.where(mine_code[s, 0, 0] > 0, weight[s, 0], 0.0) for s in range(N_MIC)]
        return correlation, weights

    def update(weights, source, low, high):
        places = [place_of(s) for s in range(N_MIC)]
        before = []
        for s in range(N_MIC):
            index = jnp.int32(N_MIC)
            for other in range(s):
                index = jnp.where(places[other] == places[s], other, index)
            before.append(index)
        last = []
        for p in range(OWN):
            index = jnp.int32(N_MIC)
            for s in range(N_MIC):
                index = jnp.where(places[s] == p, s, index)
            last.append(index)

        @pl.loop(low, high)
        def _(i):
            rows = pl.ds(pl.multiple_of(i * ROWS, ROWS), ROWS)
            for s in range(N_MIC):
                table = ctf[s, rows, :]
                scaled = weights[s] * table
                term = (scaled * owned[s, rows, :].astype(jnp.float32)).astype(jnp.bfloat16).astype(jnp.float32)
                total[0, s] = term + total[0, before[s]]
                total[1, s] = scaled * table + total[1, before[s]]
            for p in range(OWN):
                top = total[0, last[p]] + PRIOR_WEIGHT * source[p, rows, :].astype(jnp.float32)
                out_ref[p, rows, :] = (top / (total[1, last[p]] + PRIOR_WEIGHT)).astype(jnp.bfloat16)

    plane_labels, mine_labels = [], []
    for step in range(1, CHUNKS + half + LAG + 2):
        if half < step <= half + CHUNKS:
            to_plane(step - half - 1)
        if half + LAG < step <= half + LAG + CHUNKS:
            to_owner(step - half - LAG - 1)
        for c in range(CHUNKS):
            if 1 <= step - c <= half:
                hop(c, step - c)
        if step == 3:
            choose_line()
            plane_labels += [
                send(pack_label.at[d - 1], plane_label.at[N_Y - d], yl_send.at[d - 1], yl_recv.at[d - 1], at_y(d))
                for d in range(1, N_Y)
            ]
        if step == 4:
            for copy in plane_labels:
                copy.wait_recv()
            choose_plane()
            mine_labels += [
                send(parcel_label.at[d - 1], mine_label.at[N_MIC - d], ml_send.at[d - 1], ml_recv.at[d - 1], at_mic(d))
                for d in range(1, N_MIC)
            ]
        if step == 6:
            tables()
        if half + LAG + 1 < step:
            c = step - half - LAG - 2
            for d in range(1, N_MIC):
                m_copies[c, d].wait_recv()
            collect(STARTS[c], DEPTHS[c], refs_ref, True)

    _, weights = correlate()
    update(weights, refs_ref, 0, SIDE // ROWS)
    for s in range(N_MIC):
        for n in range(2):
            sums[s, n] = jnp.zeros((8, SIDE), jnp.float32)
    collect(0, SIDE, out_ref, False)
    correlation, weights = correlate()

    for s in range(N_MIC):
        tile = jnp.broadcast_to(correlation[s : s + 1, :], (8, 128))
        if s == 0:
            row[0] = tile
        else:
            row_scores[s - 1] = tile
    by_mic = [
        send(row_scores.at[d - 1], row.at[N_MIC - d], am_send.at[d - 1], am_recv.at[d - 1], at_mic(d))
        for d in range(1, N_MIC)
    ]
    update(weights, out_ref, 0, SIDE // ROWS // 2)
    for copy in by_mic:
        copy.wait_recv()
    for d in range(N_MIC):
        plane_scores[0, pl.ds(d, 1), :] = row[d, 0:1, :]
    by_y = [
        send(plane_scores.at[0], plane_scores.at[N_Y - d], ay_send.at[d - 1], ay_recv.at[d - 1], at_y(d))
        for d in range(1, N_Y)
    ]
    update(weights, out_ref, SIDE // ROWS // 2, SIDE // ROWS)
    for copy in by_y:
        copy.wait_recv()
    line_scores[0] = plane_scores[...]
    by_z = [
        send(plane_scores, line_scores.at[N_Z - d], az_send.at[d - 1], az_recv.at[d - 1], at_z(d))
        for d in range(1, N_Z)
    ]
    for copy in by_z:
        copy.wait_recv()
    lane = lax.broadcasted_iota(jnp.int32, (8, 128), 1)
    scores = jnp.zeros((8, 128), jnp.float32)
    for j in range(MINE):
        owner = bin_place_ref[bin_ref[j]] >> 3
        away_z = ((owner >> 2) - z) & (N_Z - 1)
        away_y = (owner - y) & (N_Y - 1)
        away_mic = ((owner >> 5) - mic) & (N_MIC - 1)
        scores = jnp.where(lane == j, line_scores[away_z, away_y, pl.ds(away_mic, 1), :], scores)
    score_ref[...] = scores
    for copy in copies:
        copy.wait_send()


def body(images, offsets, ctf_group, particle_bin, bin_place, defocus, bfactor, references):
    smem = pl.BlockSpec(memory_space=pltpu.SMEM)
    vmem = pl.BlockSpec(memory_space=pltpu.VMEM)
    buffers = [pltpu.VMEM((n, depth, SIDE), jnp.bfloat16)
               for n in (N_Z * MINE, (N_Y - 1) * MINE, N_Y * MINE, N_MIC - 1) for depth in DEPTHS]
    labels = [pltpu.VMEM((n, 8, 128), jnp.int32) for n in (N_Z, N_Y - 1, N_Y, N_MIC - 1, N_MIC)]
    codes = [pltpu.SMEM((n, 8, 128), jnp.int32) for n in (N_Z, N_Y, N_MIC)]
    dma = pltpu.SemaphoreType.DMA
    sems = [dma(shape) for shape in ((CHUNKS, 2, N_Z // 2), (CHUNKS, N_Y - 1), (CHUNKS, N_MIC - 1),
                                     (N_Z - 1,), (N_Y - 1,), (N_MIC - 1,),
                                     (N_MIC - 1,), (N_Y - 1,), (N_Z - 1,)) for _ in range(2)]
    f32 = [pltpu.VMEM(shape, jnp.float32) for shape in (
        (N_MIC, SIDE, SIDE), (N_MIC, 3, 8, SIDE), (2, N_MIC + 1, ROWS, SIDE),
        (N_MIC - 1, 8, 128), (N_MIC, 8, 128), (N_Y, 8, 128), (N_Z, N_Y, 8, 128))]
    refined, scores = pl.pallas_call(
        kernel,
        out_shape=(
            jax.ShapeDtypeStruct((OWN, SIDE, SIDE), jnp.bfloat16),
            jax.ShapeDtypeStruct((8, 128), jnp.float32),
        ),
        in_specs=[smem] * 6 + [vmem] * 3,
        out_specs=(vmem, vmem),
        scratch_shapes=buffers + labels + codes + sems + [dma((3,))]
        + [pltpu.VMEM((MINE, SIDE, SIDE), jnp.bfloat16), pltpu.VMEM((N_MIC, SIDE, SIDE), jnp.bfloat16)] + f32,
        compiler_params=pltpu.CompilerParams(
            collective_id=0, has_side_effects=True, vmem_limit_bytes=32 << 20
        ),
        name="project",
    )(particle_bin, bin_place, ctf_group, offsets, defocus, bfactor, hartley(SIDE), images, references)
    return (refined, scores[0, :MINE])


def solution(mesh):
    tiles, items = P(("mic", "bin"), None, None), P(("mic", "bin"))
    return jax.shard_map(
        body,
        mesh=mesh,
        in_specs=(tiles, P(None, ("mic", "bin")), items, items, P(), P(), P(), tiles),
        out_specs=(tiles, items),
        check_vma=False,
    )
```

```python
import math

import jax
import jax.numpy as jnp
import ml_dtypes
import numpy as np
from jax import lax
from jax.experimental import pallas as pl
from jax.experimental.pallas import tpu as pltpu
from jax.sharding import PartitionSpec as P

PRIOR_WEIGHT = 0.5
EPSILON = 1e-06
CONTRAST = 0.1
AMPLITUDE = math.sqrt(1.0 - CONTRAST * CONTRAST)
SIDE = 256
PIXELS = SIDE * SIDE
N_MIC, N_BIN, N_Z, N_Y = 8, 32, 8, 4
OWN, MINE = 8, 4
ROWS = 32
CTF_GROUPS = 64
DEPTHS = (64, 64, 64, 32, 32)
CHUNKS = len(DEPTHS)
STARTS = [sum(DEPTHS[:c]) for c in range(CHUNKS)]
HOP, PLANE, OWNER = 0, 1, 2
ORDER = (
    (HOP, 2, 1), (HOP, 0, 1), (HOP, 1, 1), (HOP, 0, 2), (HOP, 1, 2), (HOP, 0, 3),
    (HOP, 1, 3), (HOP, 0, 4), (HOP, 2, 2), (HOP, 1, 4), (PLANE, 0, 0), (HOP, 3, 1),
    (HOP, 2, 3), (PLANE, 1, 0), (HOP, 4, 1), (HOP, 3, 2), (HOP, 2, 4), (HOP, 4, 2),
    (HOP, 3, 3), (PLANE, 2, 0), (HOP, 4, 3), (HOP, 3, 4), (OWNER, 1, 0), (HOP, 4, 4),
    (PLANE, 3, 0), (OWNER, 0, 0), (PLANE, 4, 0), (OWNER, 2, 0), (OWNER, 3, 0), (OWNER, 4, 0),
)
LABELS_AT = 10
MESH = pl.DeviceIdType.MESH


def hartley():
    k = np.arange(SIDE)
    angles = (np.outer(k, k) % SIDE).astype(np.float32) * np.float32(2.0 * math.pi / SIDE)
    return ((np.cos(angles) + np.sin(angles)) / np.float32(math.sqrt(SIDE))).astype(ml_dtypes.bfloat16)


def code_of(bin_ref, place_ref, group_ref, j):
    return place_ref[bin_ref[j]] * CTF_GROUPS + group_ref[j] + 1


def lanes_of(values):
    lane = lax.broadcasted_iota(jnp.int32, (8, 128), 1)
    tile = jnp.zeros((8, 128), jnp.int32)
    for j, value in enumerate(values):
        tile = jnp.where(lane == j, value, tile)
    return tile


def transform(offset_ref, basis_ref, images_ref, spectra):
    r = lax.broadcasted_iota(jnp.int32, (SIDE, SIDE), 0)
    c = lax.broadcasted_iota(jnp.int32, (SIDE, SIDE), 1)

    def one_hot(mask):
        return jnp.where(mask, 1.0, 0.0).astype(jnp.bfloat16)

    def dot(a, b):
        return jnp.dot(a, b, preferred_element_type=jnp.float32).astype(jnp.bfloat16)

    for j in range(MINE):
        moved = dot(one_hot(c == ((r + offset_ref[0, j]) & (SIDE - 1))), images_ref[j])
        moved = dot(moved, one_hot(r == ((c + offset_ref[1, j]) & (SIDE - 1))))
        spectra[j] = dot(dot(basis_ref[...], moved), basis_ref[...])


def kernel(*refs):
    inputs, (out_ref, score_ref), scratch = refs[:9], refs[9:11], refs[20:]
    bin_ref, bin_place_ref, group_ref, offset_ref, focus_ref, damp_ref, basis_ref, images_ref, refs_ref = held = refs[11:20]
    lines, packs = scratch[:CHUNKS], scratch[CHUNKS : 2 * CHUNKS]
    planes, parcels = scratch[2 * CHUNKS : 3 * CHUNKS], scratch[3 * CHUNKS : 4 * CHUNKS]
    (line_label, pack_label, plane_label, parcel_label, mine_label, line_code, plane_code, mine_code,
     z_send, z_recv, y_send, y_recv, m_send, m_recv, zl_send, zl_recv, yl_send, yl_recv,
     ml_send, ml_recv, am_send, am_recv, ay_send, ay_recv, az_send, az_recv, code_sem,
     load_sem, spectra, owned, ctf, sums, total, row_scores, row, plane_scores, line_scores) = scratch[4 * CHUNKS :]
    mic, column = lax.axis_index("mic"), lax.axis_index("bin")
    z, y = column >> 2, column & (N_Y - 1)

    def at_z(d):
        return (mic, (((z + d) & (N_Z - 1)) << 2) + y)

    def at_y(d):
        return (mic, (z << 2) + ((y + d) & (N_Y - 1)))

    def at_mic(d):
        return ((mic + d) & (N_MIC - 1), column)

    def send(src, dst, send_sem, recv_sem, peer):
        copy = pltpu.make_async_remote_copy(
            src_ref=src, dst_ref=dst, send_sem=send_sem, recv_sem=recv_sem,
            device_id=peer, device_id_type=MESH,
        )
        copy.start()
        copies.append(copy)
        return copy

    copies = []
    loads = [
        pltpu.make_async_copy(src, dst, load_sem.at[n])
        for n, (src, dst) in enumerate(zip(inputs, held))
    ]
    for load in loads:
        load.start()
    peers = [at_z(d) for d in range(1, N_Z)] + [at_y(d) for d in range(1, N_Y)] + [at_mic(d) for d in range(1, N_MIC)]
    barrier = pltpu.get_barrier_semaphore()
    for peer in peers:
        pl.semaphore_signal(barrier, inc=1, device_id=peer, device_id_type=MESH)
    for load in loads[:8]:
        load.wait()
    transform(offset_ref, basis_ref, images_ref, spectra)
    for block in range(2):
        total[block, N_MIC] = jnp.zeros((ROWS, SIDE), jnp.float32)
    sums[...] = jnp.zeros_like(sums)
    pl.semaphore_wait(barrier, len(peers))


    hops, y_copies, m_copies = {}, {}, {}
    pick_line, pick_plane = [], []
    half = N_Z // 2

    def hop(c, h):
        line = lines[c]
        if h == 1:
            line[0:MINE] = spectra[:, STARTS[c] : STARTS[c] + DEPTHS[c], :]
        for way in range(2):
            if h > 1:
                hops[c, way, h - 1].wait_recv()
            src = (1 - h) % N_Z if way == 0 else h - 1
            dst = N_Z - h if way == 0 else h
            low, count = 0, MINE
            if h == half:
                low, count = (MINE // 2) * way, MINE // 2
            hops[c, way, h] = send(
                line.at[pl.ds(src * MINE + low, count)], line.at[pl.ds(dst * MINE + low, count)],
                z_send.at[c, way, h - 1], z_recv.at[c, way, h - 1], at_z(1 if way == 0 else N_Z - 1),
            )

    def choose_line():
        for copy in line_labels:
            copy.wait_recv()
        fetch = pltpu.make_async_copy(line_label, line_code, code_sem.at[0])
        fetch.start()
        fetch.wait()
        keys = [[jnp.int32(0)] * MINE for _ in range(N_Y)]
        counts = [jnp.int32(0)] * N_Y
        for t in range(N_Z * MINE):
            code = line_code[t // MINE, 0, t % MINE]
            owner = (code - 1) >> 9
            here = ((owner >> 2) & (N_Z - 1)) == z
            away = (owner - y) & (N_Y - 1)
            key = code * (N_Z * MINE) + t
            for d in range(N_Y):
                hit = here & (away == d)
                rank = jnp.where(hit, counts[d], MINE)
                counts[d] = counts[d] + jnp.where(hit, 1, 0)
                keys[d] = [jnp.where(rank == k, key, keys[d][k]) for k in range(MINE)]
        pick_line.extend([[key & (N_Z * MINE - 1) for key in keys[d]] for d in range(N_Y)])
        for d in range(N_Y):
            tile = lanes_of([key >> 5 for key in keys[d]])
            if d == 0:
                plane_label[0] = tile
            else:
                pack_label[d - 1] = tile

    def to_plane(c):
        for way in range(2):
            hops[c, way, half].wait_recv()
        for d in range(N_Y):
            for k in range(MINE):
                tile = lines[c][pick_line[d][k]]
                if d == 0:
                    planes[c][k] = tile
                else:
                    packs[c][(d - 1) * MINE + k] = tile
        for d in range(1, N_Y):
            y_copies[c, d] = send(
                packs[c].at[pl.ds((d - 1) * MINE, MINE)], planes[c].at[pl.ds((N_Y - d) * MINE, MINE)],
                y_send.at[c, d - 1], y_recv.at[c, d - 1], at_y(d),
            )

    def choose_plane():
        fetch = pltpu.make_async_copy(plane_label, plane_code, code_sem.at[1])
        fetch.start()
        fetch.wait()
        keys = [jnp.int32(0)] * N_MIC
        for s in range(N_Y * MINE):
            code = plane_code[s // MINE, 0, s % MINE]
            away = (((code - 1) >> 14) - mic) & (N_MIC - 1)
            away = jnp.where(code > 0, away, N_MIC)
            key = code * (N_Y * MINE) + s
            keys = [jnp.where(away == d, key, keys[d]) for d in range(N_MIC)]
        pick_plane.extend([key & (N_Y * MINE - 1) for key in keys])
        for d in range(N_MIC):
            tile = jnp.full((8, 128), keys[d] >> 4, jnp.int32)
            if d == 0:
                mine_label[0] = tile
            else:
                parcel_label[d - 1] = tile

    def to_owner(c):
        for d in range(1, N_Y):
            y_copies[c, d].wait_recv()
        rows = pl.ds(STARTS[c], DEPTHS[c])
        for d in range(N_MIC):
            tile = planes[c][pick_plane[d]]
            if d == 0:
                owned[0, rows, :] = tile
            else:
                parcels[c][d - 1] = tile
        for d in range(1, N_MIC):
            m_copies[c, d] = send(
                parcels[c].at[d - 1], owned.at[N_MIC - d, rows, :],
                m_send.at[c, d - 1], m_recv.at[c, d - 1], at_mic(d),
            )

    line_label[0] = lanes_of([code_of(bin_ref, bin_place_ref, group_ref, j) for j in range(MINE)])
    line_labels = [
        send(line_label.at[0], line_label.at[N_Z - d], zl_send.at[d - 1], zl_recv.at[d - 1], at_z(d))
        for d in range(1, N_Z)
    ]
    def place_of(s):
        return ((mine_code[s, 0, 0] - 1) >> 6) & (OWN - 1)

    def tables(mine_labels):
        for copy in mine_labels:
            copy.wait_recv()
        fetch = pltpu.make_async_copy(mine_label, mine_code, code_sem.at[2])
        fetch.start()
        fetch.wait()
        slot = lax.broadcasted_iota(jnp.int32, (N_MIC, SIDE), 0)
        focus = jnp.zeros((N_MIC, SIDE), jnp.float32)
        damp = jnp.zeros((N_MIC, SIDE), jnp.float32)
        for s in range(N_MIC):
            group = (mine_code[s, 0, 0] - 1) & (CTF_GROUPS - 1)
            focus = jnp.where(slot == s, focus_ref[group], focus)
            damp = jnp.where(slot == s, damp_ref[group], damp)
        k = lax.broadcasted_iota(jnp.int32, (N_MIC, SIDE), 1)
        folded = jnp.minimum(k, SIDE - k).astype(jnp.float32) * (2.0 / SIDE)
        square = folded * folded
        sine, cosine = jnp.sin(focus * square), jnp.cos(focus * square)
        envelope = jnp.exp(-damp * square)
        row_sine = jnp.transpose(-sine * envelope)
        row_cosine = jnp.transpose(-cosine * envelope)
        col_sine = (AMPLITUDE * cosine - CONTRAST * sine) * envelope
        col_cosine = (AMPLITUDE * sine + CONTRAST * cosine) * envelope
        for s in range(N_MIC):
            ctf[s] = (
                row_sine[:, s : s + 1] * col_sine[s : s + 1, :]
                + row_cosine[:, s : s + 1] * col_cosine[s : s + 1, :]
            )

    def collect(start, depth, source, with_data):
        @pl.loop(0, N_MIC)
        def _(s):
            place = place_of(s)
            parts = [jnp.zeros((16, SIDE), jnp.float32)] * 3
            for low in range(start, start + depth, 16):
                rows = pl.ds(low, 16)
                predicted = ctf[s, rows, :] * source[place, rows, :].astype(jnp.float32)
                values = owned[s, rows, :].astype(jnp.float32)
                parts[0] = parts[0] + predicted * values
                parts[1] = parts[1] + predicted * predicted
                if with_data:
                    parts[2] = parts[2] + values * values
            for n in range(3 if with_data else 2):
                sums[s, n] += parts[n][:8] + parts[n][8:]

    def correlate():
        slot = lax.broadcasted_iota(jnp.int32, (N_MIC, 128), 0)
        means = []
        for n in range(3):
            mean = jnp.zeros((N_MIC, 128), jnp.float32)
            for s in range(N_MIC):
                mean = jnp.where(slot == s, jnp.sum(sums[s, n], keepdims=True), mean)
            means.append(mean / PIXELS)
        correlation = means[0] / jnp.sqrt((means[1] + EPSILON) * (means[2] + EPSILON))
        weight = 1.0 / (1.0 + jnp.exp(-SIDE * correlation))
        weight = weight.astype(jnp.bfloat16).astype(jnp.float32)
        weights = [jnp.where(mine_code[s, 0, 0] > 0, weight[s, 0], 0.0) for s in range(N_MIC)]
        return correlation, weights

    def update(weights, source, low, high):
        places = [place_of(s) for s in range(N_MIC)]
        before = []
        for s in range(N_MIC):
            index = jnp.int32(N_MIC)
            for other in range(s):
                index = jnp.where(places[other] == places[s], other, index)
            before.append(index)
        last = []
        for p in range(OWN):
            index = jnp.int32(N_MIC)
            for s in range(N_MIC):
                index = jnp.where(places[s] == p, s, index)
            last.append(index)

        @pl.loop(low, high)
        def _(i):
            rows = pl.ds(pl.multiple_of(i * ROWS, ROWS), ROWS)
            for s in range(N_MIC):
                table = ctf[s, rows, :]
                scaled = weights[s] * table
                term = (scaled * owned[s, rows, :].astype(jnp.float32)).astype(jnp.bfloat16).astype(jnp.float32)
                total[0, s] = term + total[0, before[s]]
                total[1, s] = scaled * table + total[1, before[s]]
            for p in range(OWN):
                top = total[0, last[p]] + PRIOR_WEIGHT * source[p, rows, :].astype(jnp.float32)
                out_ref[p, rows, :] = (top / (total[1, last[p]] + PRIOR_WEIGHT)).astype(jnp.bfloat16)

    owners_done = []
    for n, (kind, c, h) in enumerate(ORDER):
        if n == LABELS_AT:
            choose_line()
            plane_labels = [
                send(pack_label.at[d - 1], plane_label.at[N_Y - d], yl_send.at[d - 1], yl_recv.at[d - 1], at_y(d))
                for d in range(1, N_Y)
            ]
        if kind == HOP:
            hop(c, h)
        elif kind == PLANE:
            to_plane(c)
        else:
            if not owners_done:
                for copy in plane_labels:
                    copy.wait_recv()
                choose_plane()
                mine_labels = [
                    send(parcel_label.at[d - 1], mine_label.at[N_MIC - d], ml_send.at[d - 1], ml_recv.at[d - 1], at_mic(d))
                    for d in range(1, N_MIC)
                ]
            to_owner(c)
            owners_done.append(c)
            if len(owners_done) == CHUNKS - 1:
                tables(mine_labels)
    loads[8].wait()
    for c in owners_done:
        for d in range(1, N_MIC):
            m_copies[c, d].wait_recv()
        collect(STARTS[c], DEPTHS[c], refs_ref, True)

    _, weights = correlate()
    update(weights, refs_ref, 0, SIDE // ROWS)
    for s in range(N_MIC):
        for n in range(2):
            sums[s, n] = jnp.zeros((8, SIDE), jnp.float32)
    collect(0, SIDE, out_ref, False)
    correlation, weights = correlate()

    for s in range(N_MIC):
        tile = jnp.broadcast_to(correlation[s : s + 1, :], (8, 128))
        if s == 0:
            row[0] = tile
        else:
            row_scores[s - 1] = tile
    by_mic = [
        send(row_scores.at[d - 1], row.at[N_MIC - d], am_send.at[d - 1], am_recv.at[d - 1], at_mic(d))
        for d in range(1, N_MIC)
    ]
    update(weights, out_ref, 0, SIDE // ROWS // 2)
    for copy in by_mic:
        copy.wait_recv()
    for d in range(N_MIC):
        plane_scores[0, pl.ds(d, 1), :] = row[d, 0:1, :]
    by_y = [
        send(plane_scores.at[0], plane_scores.at[N_Y - d], ay_send.at[d - 1], ay_recv.at[d - 1], at_y(d))
        for d in range(1, N_Y)
    ]
    update(weights, out_ref, SIDE // ROWS // 2, SIDE // ROWS)
    for copy in by_y:
        copy.wait_recv()
    line_scores[0] = plane_scores[...]
    by_z = [
        send(plane_scores, line_scores.at[N_Z - d], az_send.at[d - 1], az_recv.at[d - 1], at_z(d))
        for d in range(1, N_Z)
    ]
    for copy in by_z:
        copy.wait_recv()
    lane = lax.broadcasted_iota(jnp.int32, (8, 128), 1)
    scores = jnp.zeros((8, 128), jnp.float32)
    for j in range(MINE):
        owner = bin_place_ref[bin_ref[j]] >> 3
        away_z = ((owner >> 2) - z) & (N_Z - 1)
        away_y = (owner - y) & (N_Y - 1)
        away_mic = ((owner >> 5) - mic) & (N_MIC - 1)
        scores = jnp.where(lane == j, line_scores[away_z, away_y, pl.ds(away_mic, 1), :], scores)
    score_ref[...] = scores
    for copy in copies:
        copy.wait_send()


def body(images, offsets, ctf_group, particle_bin, bin_place, defocus, bfactor, references):
    inputs = (particle_bin, bin_place, ctf_group, offsets, defocus, bfactor, jnp.asarray(hartley()), images, references)
    held = [(pltpu.SMEM if n < 6 else pltpu.VMEM)(x.shape, x.dtype) for n, x in enumerate(inputs)]
    vmem = pl.BlockSpec(memory_space=pltpu.VMEM)
    buffers = [pltpu.VMEM((n, depth, SIDE), jnp.bfloat16)
               for n in (N_Z * MINE, (N_Y - 1) * MINE, N_Y * MINE, N_MIC - 1) for depth in DEPTHS]
    labels = [pltpu.VMEM((n, 8, 128), jnp.int32) for n in (N_Z, N_Y - 1, N_Y, N_MIC - 1, N_MIC)]
    codes = [pltpu.SMEM((n, 8, 128), jnp.int32) for n in (N_Z, N_Y, N_MIC)]
    dma = pltpu.SemaphoreType.DMA
    sems = [dma(shape) for shape in ((CHUNKS, 2, N_Z // 2), (CHUNKS, N_Y - 1), (CHUNKS, N_MIC - 1),
                                     (N_Z - 1,), (N_Y - 1,), (N_MIC - 1,),
                                     (N_MIC - 1,), (N_Y - 1,), (N_Z - 1,)) for _ in range(2)]
    f32 = [pltpu.VMEM(shape, jnp.float32) for shape in (
        (N_MIC, SIDE, SIDE), (N_MIC, 3, 8, SIDE), (2, N_MIC + 1, ROWS, SIDE),
        (N_MIC - 1, 8, 128), (N_MIC, 8, 128), (N_Y, 8, 128), (N_Z, N_Y, 8, 128))]
    refined, scores = pl.pallas_call(
        kernel,
        out_shape=(
            jax.ShapeDtypeStruct((OWN, SIDE, SIDE), jnp.bfloat16),
            jax.ShapeDtypeStruct((8, 128), jnp.float32),
        ),
        in_specs=[pl.BlockSpec(memory_space=pltpu.HBM)] * 9,
        out_specs=(vmem, vmem),
        scratch_shapes=held + buffers + labels + codes + sems + [dma((3,))]
+ [dma((9,))]
        + [pltpu.VMEM((MINE, SIDE, SIDE), jnp.bfloat16), pltpu.VMEM((N_MIC, SIDE, SIDE), jnp.bfloat16)] + f32,
        compiler_params=pltpu.CompilerParams(
            collective_id=0, has_side_effects=True, vmem_limit_bytes=32 << 20
        ),
        name="project",
    )(*[pltpu.with_memory_space_constraint(x, pltpu.HBM) for x in inputs])
    return (refined, scores[0, :MINE])


def solution(mesh):
    tiles, items = P(("mic", "bin"), None, None), P(("mic", "bin"))
    return jax.shard_map(
        body,
        mesh=mesh,
        in_specs=(tiles, P(None, ("mic", "bin")), items, items, P(), P(), P(), tiles),
        out_specs=(tiles, items),
        check_vma=False,
    )
```

```python
import math

import jax
import jax.numpy as jnp
import ml_dtypes
import numpy as np
from jax import lax
from jax.experimental import pallas as pl
from jax.experimental.pallas import tpu as pltpu
from jax.sharding import PartitionSpec as P

PRIOR_WEIGHT = 0.5
EPSILON = 1e-06
CONTRAST = 0.1
AMPLITUDE = math.sqrt(1.0 - CONTRAST * CONTRAST)
SIDE = 256
PIXELS = SIDE * SIDE
N_MIC, N_BIN, N_Z, N_Y = 8, 32, 8, 4
OWN, MINE = 8, 4
ROWS = 32
CTF_GROUPS = 64
DEPTHS = (64, 64, 64, 32, 32)
CHUNKS = len(DEPTHS)
STARTS = [sum(DEPTHS[:c]) for c in range(CHUNKS)]
HOP, PLANE, OWNER = 0, 1, 2
ORDER = (
    (HOP, 2, 1), (HOP, 0, 1), (HOP, 1, 1), (HOP, 0, 2), (HOP, 1, 2), (HOP, 0, 3),
    (HOP, 1, 3), (HOP, 0, 4), (HOP, 2, 2), (HOP, 1, 4), (PLANE, 0, 0), (HOP, 3, 1),
    (HOP, 2, 3), (PLANE, 1, 0), (HOP, 4, 1), (HOP, 3, 2), (HOP, 2, 4), (HOP, 4, 2),
    (HOP, 3, 3), (PLANE, 2, 0), (HOP, 4, 3), (HOP, 3, 4), (OWNER, 1, 0), (HOP, 4, 4),
    (PLANE, 3, 0), (OWNER, 0, 0), (PLANE, 4, 0), (OWNER, 2, 0), (OWNER, 3, 0), (OWNER, 4, 0),
)
LABELS_AT = (6, 7, 11, 12, 16, 19)
MESH = pl.DeviceIdType.MESH


def hartley():
    k = np.arange(SIDE)
    angles = (np.outer(k, k) % SIDE).astype(np.float32) * np.float32(2.0 * math.pi / SIDE)
    return ((np.cos(angles) + np.sin(angles)) / np.float32(math.sqrt(SIDE))).astype(ml_dtypes.bfloat16)


def code_of(bin_ref, place_ref, group_ref, j):
    return place_ref[bin_ref[j]] * CTF_GROUPS + group_ref[j] + 1


def lanes_of(values):
    lane = lax.broadcasted_iota(jnp.int32, (8, 128), 1)
    tile = jnp.zeros((8, 128), jnp.int32)
    for j, value in enumerate(values):
        tile = jnp.where(lane == j, value, tile)
    return tile


def transform(offset_ref, basis_ref, images_ref, spectra):
    r = lax.broadcasted_iota(jnp.int32, (SIDE, SIDE), 0)
    c = lax.broadcasted_iota(jnp.int32, (SIDE, SIDE), 1)

    def one_hot(mask):
        return jnp.where(mask, 1.0, 0.0).astype(jnp.bfloat16)

    def dot(a, b):
        return jnp.dot(a, b, preferred_element_type=jnp.float32).astype(jnp.bfloat16)

    for j in range(MINE):
        moved = dot(one_hot(c == ((r + offset_ref[0, j]) & (SIDE - 1))), images_ref[j])
        moved = dot(moved, one_hot(r == ((c + offset_ref[1, j]) & (SIDE - 1))))
        spectra[j] = dot(dot(basis_ref[...], moved), basis_ref[...])


def kernel(*refs):
    inputs, (out_ref, score_ref), scratch = refs[:9], refs[9:11], refs[20:]
    bin_ref, bin_place_ref, group_ref, offset_ref, focus_ref, damp_ref, basis_ref, images_ref, refs_ref = held = refs[11:20]
    lines, packs = scratch[:CHUNKS], scratch[CHUNKS : 2 * CHUNKS]
    planes, parcels = scratch[2 * CHUNKS : 3 * CHUNKS], scratch[3 * CHUNKS : 4 * CHUNKS]
    (line_label, pack_label, plane_label, parcel_label, mine_label, line_code, plane_code, mine_code,
     z_send, z_recv, y_send, y_recv, m_send, m_recv, zl_send, zl_recv, yl_send, yl_recv,
     ml_send, ml_recv, am_send, am_recv, ay_send, ay_recv, az_send, az_recv, code_sem,
     load_sem, spectra, owned, ctf, sums, total, row_scores, row, plane_scores, line_scores) = scratch[4 * CHUNKS :]
    mic, column = lax.axis_index("mic"), lax.axis_index("bin")
    z, y = column >> 2, column & (N_Y - 1)

    def at_z(d):
        return (mic, (((z + d) & (N_Z - 1)) << 2) + y)

    def at_y(d):
        return (mic, (z << 2) + ((y + d) & (N_Y - 1)))

    def at_mic(d):
        return ((mic + d) & (N_MIC - 1), column)

    def send(src, dst, send_sem, recv_sem, peer):
        copy = pltpu.make_async_remote_copy(
            src_ref=src, dst_ref=dst, send_sem=send_sem, recv_sem=recv_sem,
            device_id=peer, device_id_type=MESH,
        )
        copy.start()
        copies.append(copy)
        return copy

    copies = []
    loads = [
        pltpu.make_async_copy(src, dst, load_sem.at[n])
        for n, (src, dst) in enumerate(zip(inputs, held))
    ]
    for load in loads:
        load.start()
    peers = [at_z(d) for d in range(1, N_Z)] + [at_y(d) for d in range(1, N_Y)] + [at_mic(d) for d in range(1, N_MIC)]
    barrier = pltpu.get_barrier_semaphore()
    for peer in peers:
        pl.semaphore_signal(barrier, inc=1, device_id=peer, device_id_type=MESH)
    for load in loads[:8]:
        load.wait()
    transform(offset_ref, basis_ref, images_ref, spectra)
    for block in range(2):
        total[block, N_MIC] = jnp.zeros((ROWS, SIDE), jnp.float32)
    sums[...] = jnp.zeros_like(sums)
    pl.semaphore_wait(barrier, len(peers))


    hops, y_copies, m_copies = {}, {}, {}
    pick_line, pick_plane = [], []
    half = N_Z // 2

    def hop(c, h):
        line = lines[c]
        if h == 1:
            line[0:MINE] = spectra[:, STARTS[c] : STARTS[c] + DEPTHS[c], :]
        for way in range(2):
            if h > 1:
                hops[c, way, h - 1].wait_recv()
            src = (1 - h) % N_Z if way == 0 else h - 1
            dst = N_Z - h if way == 0 else h
            low, count = 0, MINE
            if h == half:
                low, count = (MINE // 2) * way, MINE // 2
            hops[c, way, h] = send(
                line.at[pl.ds(src * MINE + low, count)], line.at[pl.ds(dst * MINE + low, count)],
                z_send.at[c, way, h - 1], z_recv.at[c, way, h - 1], at_z(1 if way == 0 else N_Z - 1),
            )

    def choose_line():
        keys = [[jnp.int32(0)] * MINE for _ in range(N_Y)]
        counts = [jnp.int32(0)] * N_Y
        for t in range(N_Z * MINE):
            code = line_code[t // MINE, 0, t % MINE]
            owner = (code - 1) >> 9
            here = ((owner >> 2) & (N_Z - 1)) == z
            away = (owner - y) & (N_Y - 1)
            key = code * (N_Z * MINE) + t
            for d in range(N_Y):
                hit = here & (away == d)
                rank = jnp.where(hit, counts[d], MINE)
                counts[d] = counts[d] + jnp.where(hit, 1, 0)
                keys[d] = [jnp.where(rank == k, key, keys[d][k]) for k in range(MINE)]
        pick_line.extend([[key & (N_Z * MINE - 1) for key in keys[d]] for d in range(N_Y)])
        for d in range(N_Y):
            tile = lanes_of([key >> 5 for key in keys[d]])
            if d == 0:
                plane_label[0] = tile
            else:
                pack_label[d - 1] = tile

    def to_plane(c):
        for way in range(2):
            hops[c, way, half].wait_recv()
        for d in range(N_Y):
            for k in range(MINE):
                tile = lines[c][pick_line[d][k]]
                if d == 0:
                    planes[c][k] = tile
                else:
                    packs[c][(d - 1) * MINE + k] = tile
        for d in range(1, N_Y):
            y_copies[c, d] = send(
                packs[c].at[pl.ds((d - 1) * MINE, MINE)], planes[c].at[pl.ds((N_Y - d) * MINE, MINE)],
                y_send.at[c, d - 1], y_recv.at[c, d - 1], at_y(d),
            )

    def choose_plane():
        keys = [jnp.int32(0)] * N_MIC
        for s in range(N_Y * MINE):
            code = plane_code[s // MINE, 0, s % MINE]
            away = (((code - 1) >> 14) - mic) & (N_MIC - 1)
            away = jnp.where(code > 0, away, N_MIC)
            key = code * (N_Y * MINE) + s
            keys = [jnp.where(away == d, key, keys[d]) for d in range(N_MIC)]
        pick_plane.extend([key & (N_Y * MINE - 1) for key in keys])
        for d in range(N_MIC):
            tile = jnp.full((8, 128), keys[d] >> 4, jnp.int32)
            if d == 0:
                mine_label[0] = tile
            else:
                parcel_label[d - 1] = tile

    def to_owner(c):
        for d in range(1, N_Y):
            y_copies[c, d].wait_recv()
        rows = pl.ds(STARTS[c], DEPTHS[c])
        for d in range(N_MIC):
            tile = planes[c][pick_plane[d]]
            if d == 0:
                owned[0, rows, :] = tile
            else:
                parcels[c][d - 1] = tile
        for d in range(1, N_MIC):
            m_copies[c, d] = send(
                parcels[c].at[d - 1], owned.at[N_MIC - d, rows, :],
                m_send.at[c, d - 1], m_recv.at[c, d - 1], at_mic(d),
            )

    def read_codes(labels, label, code, n):
        for copy in labels:
            copy.wait_recv()
        fetch = pltpu.make_async_copy(label.at[:, 0:1], code.at[:, 0:1], code_sem.at[n])
        fetch.start()
        return fetch

    owners_done = []
    for n, (kind, c, h) in enumerate(ORDER):
        if n == 3:
            line_label[0] = lanes_of([code_of(bin_ref, bin_place_ref, group_ref, j) for j in range(MINE)])
            line_labels = [
                send(line_label.at[0, 0:1], line_label.at[N_Z - d, 0:1], zl_send.at[d - 1], zl_recv.at[d - 1], at_z(d))
                for d in range(1, N_Z)
            ]
            def place_of(s):
                return ((mine_code[s, 0, 0] - 1) >> 6) & (OWN - 1)
            def tables():
                slot = lax.broadcasted_iota(jnp.int32, (N_MIC, SIDE), 0)
                focus = jnp.zeros((N_MIC, SIDE), jnp.float32)
                damp = jnp.zeros((N_MIC, SIDE), jnp.float32)
                for s in range(N_MIC):
                    group = (mine_code[s, 0, 0] - 1) & (CTF_GROUPS - 1)
                    focus = jnp.where(slot == s, focus_ref[group], focus)
                    damp = jnp.where(slot == s, damp_ref[group], damp)
                k = lax.broadcasted_iota(jnp.int32, (N_MIC, SIDE), 1)
                folded = jnp.minimum(k, SIDE - k).astype(jnp.float32) * (2.0 / SIDE)
                square = folded * folded
                sine, cosine = jnp.sin(focus * square), jnp.cos(focus * square)
                envelope = jnp.exp(-damp * square)
                row_sine = jnp.transpose(-sine * envelope)
                row_cosine = jnp.transpose(-cosine * envelope)
                col_sine = (AMPLITUDE * cosine - CONTRAST * sine) * envelope
                col_cosine = (AMPLITUDE * sine + CONTRAST * cosine) * envelope
                for s in range(N_MIC):
                    ctf[s] = (
                        row_sine[:, s : s + 1] * col_sine[s : s + 1, :]
                        + row_cosine[:, s : s + 1] * col_cosine[s : s + 1, :]
                    )
            def collect(start, depth, source, with_data):
                @pl.loop(0, N_MIC)
                def _(s):
                    place = place_of(s)
                    parts = [jnp.zeros((16, SIDE), jnp.float32)] * 3
                    for low in range(start, start + depth, 16):
                        rows = pl.ds(low, 16)
                        predicted = ctf[s, rows, :] * source[place, rows, :].astype(jnp.float32)
                        values = owned[s, rows, :].astype(jnp.float32)
                        parts[0] = parts[0] + predicted * values
                        parts[1] = parts[1] + predicted * predicted
                        if with_data:
                            parts[2] = parts[2] + values * values
                    for n in range(3 if with_data else 2):
                        sums[s, n] += parts[n][:8] + parts[n][8:]
            def correlate():
                slot = lax.broadcasted_iota(jnp.int32, (N_MIC, 128), 0)
                means = []
                for n in range(3):
                    mean = jnp.zeros((N_MIC, 128), jnp.float32)
                    for s in range(N_MIC):
                        mean = jnp.where(slot == s, jnp.sum(sums[s, n], keepdims=True), mean)
                    means.append(mean / PIXELS)
                correlation = means[0] / jnp.sqrt((means[1] + EPSILON) * (means[2] + EPSILON))
                weight = 1.0 / (1.0 + jnp.exp(-SIDE * correlation))
                weight = weight.astype(jnp.bfloat16).astype(jnp.float32)
                weights = [jnp.where(mine_code[s, 0, 0] > 0, weight[s, 0], 0.0) for s in range(N_MIC)]
                return correlation, weights
            def update(weights, source, low, high):
                places = [place_of(s) for s in range(N_MIC)]
                before = []
                for s in range(N_MIC):
                    index = jnp.int32(N_MIC)
                    for other in range(s):
                        index = jnp.where(places[other] == places[s], other, index)
                    before.append(index)
                last = []
                for p in range(OWN):
                    index = jnp.int32(N_MIC)
                    for s in range(N_MIC):
                        index = jnp.where(places[s] == p, s, index)
                    last.append(index)
                @pl.loop(low, high)
                def _(i):
                    rows = pl.ds(pl.multiple_of(i * ROWS, ROWS), ROWS)
                    for s in range(N_MIC):
                        table = ctf[s, rows, :]
                        scaled = weights[s] * table
                        term = (scaled * owned[s, rows, :].astype(jnp.float32)).astype(jnp.bfloat16).astype(jnp.float32)
                        total[0, s] = term + total[0, before[s]]
                        total[1, s] = scaled * table + total[1, before[s]]
                    for p in range(OWN):
                        top = total[0, last[p]] + PRIOR_WEIGHT * source[p, rows, :].astype(jnp.float32)
                        out_ref[p, rows, :] = (top / (total[1, last[p]] + PRIOR_WEIGHT)).astype(jnp.bfloat16)
        if n == LABELS_AT[0]:
            fetch = read_codes(line_labels, line_label, line_code, 0)
        if n == LABELS_AT[1]:
            fetch.wait()
            choose_line()
            plane_labels = [
                send(pack_label.at[d - 1, 0:1], plane_label.at[N_Y - d, 0:1], yl_send.at[d - 1], yl_recv.at[d - 1], at_y(d))
                for d in range(1, N_Y)
            ]
        if n == LABELS_AT[2]:
            fetch = read_codes(plane_labels, plane_label, plane_code, 1)
        if n == LABELS_AT[3]:
            fetch.wait()
            choose_plane()
            mine_labels = [
                send(parcel_label.at[d - 1, 0:1], mine_label.at[N_MIC - d, 0:1], ml_send.at[d - 1], ml_recv.at[d - 1], at_mic(d))
                for d in range(1, N_MIC)
            ]
        if n == LABELS_AT[4]:
            fetch = read_codes(mine_labels, mine_label, mine_code, 2)
        if n == LABELS_AT[5]:
            fetch.wait()
            tables()
        if kind == HOP:
            hop(c, h)
        elif kind == PLANE:
            to_plane(c)
        else:
            to_owner(c)
            owners_done.append(c)
    loads[8].wait()
    for c in owners_done:
        for d in range(1, N_MIC):
            m_copies[c, d].wait_recv()
        collect(STARTS[c], DEPTHS[c], refs_ref, True)

    _, weights = correlate()
    update(weights, refs_ref, 0, SIDE // ROWS)
    routed = len(copies)
    for s in range(N_MIC):
        for n in range(2):
            sums[s, n] = jnp.zeros((8, SIDE), jnp.float32)
    collect(0, SIDE, out_ref, False)
    correlation, weights = correlate()

    row_scores[...] = correlation
    row[0:1, :] = correlation[0:1, :]
    by_mic = [
        send(row_scores.at[d : d + 1], row.at[N_MIC - d : N_MIC - d + 1], am_send.at[d - 1], am_recv.at[d - 1], at_mic(d))
        for d in range(1, N_MIC)
    ]
    update(weights, out_ref, 0, SIDE // ROWS // 2)
    for copy in copies[:routed]:
        copy.wait_send()
    for copy in by_mic:
        copy.wait_recv()
    lane = lax.broadcasted_iota(jnp.int32, (8, 128), 1)
    of_mic = lax.broadcasted_iota(jnp.int32, (8, 128), 0)
    plane_scores[0:1, :] = jnp.sum(jnp.where(lane == of_mic, row[...], 0.0), axis=0, keepdims=True)
    by_y = [
        send(plane_scores.at[0:1], plane_scores.at[N_Y - d : N_Y - d + 1], ay_send.at[d - 1], ay_recv.at[d - 1], at_y(d))
        for d in range(1, N_Y)
    ]
    update(weights, out_ref, SIDE // ROWS // 2, SIDE // ROWS)
    for copy in by_y:
        copy.wait_recv()
    line_scores[0] = plane_scores[...]
    by_z = [
        send(plane_scores, line_scores.at[N_Z - d], az_send.at[d - 1], az_recv.at[d - 1], at_z(d))
        for d in range(1, N_Z)
    ]
    for copy in by_z:
        copy.wait_recv()
    scores = jnp.zeros((8, 128), jnp.float32)
    for j in range(MINE):
        owner = bin_place_ref[bin_ref[j]] >> 3
        away_z = ((owner >> 2) - z) & (N_Z - 1)
        away_y = (owner - y) & (N_Y - 1)
        away_mic = ((owner >> 5) - mic) & (N_MIC - 1)
        found = jnp.where(lane[0:1, :] == away_mic, line_scores[away_z, pl.ds(away_y, 1), :], 0.0)
        scores = jnp.where(lane == j, jnp.sum(found, keepdims=True), scores)
    score_ref[...] = scores
    for copy in copies[routed:]:
        copy.wait_send()


def body(images, offsets, ctf_group, particle_bin, bin_place, defocus, bfactor, references):
    inputs = (particle_bin, bin_place, ctf_group, offsets, defocus, bfactor, jnp.asarray(hartley()), images, references)
    held = [(pltpu.SMEM if n < 6 else pltpu.VMEM)(x.shape, x.dtype) for n, x in enumerate(inputs)]
    vmem = pl.BlockSpec(memory_space=pltpu.VMEM)
    buffers = [pltpu.VMEM((n, depth, SIDE), jnp.bfloat16)
               for n in (N_Z * MINE, (N_Y - 1) * MINE, N_Y * MINE, N_MIC - 1) for depth in DEPTHS]
    labels = [pltpu.VMEM((n, 8, 128), jnp.int32) for n in (N_Z, N_Y - 1, N_Y, N_MIC - 1, N_MIC)]
    codes = [pltpu.SMEM((n, 8, 128), jnp.int32) for n in (N_Z, N_Y, N_MIC)]
    dma = pltpu.SemaphoreType.DMA
    sems = [dma(shape) for shape in ((CHUNKS, 2, N_Z // 2), (CHUNKS, N_Y - 1), (CHUNKS, N_MIC - 1),
                                     (N_Z - 1,), (N_Y - 1,), (N_MIC - 1,),
                                     (N_MIC - 1,), (N_Y - 1,), (N_Z - 1,)) for _ in range(2)]
    f32 = [pltpu.VMEM(shape, jnp.float32) for shape in (
        (N_MIC, SIDE, SIDE), (N_MIC, 3, 8, SIDE), (2, N_MIC + 1, ROWS, SIDE),
        (N_MIC, 128), (N_MIC, 128), (N_Y, 128), (N_Z, N_Y, 128))]
    refined, scores = pl.pallas_call(
        kernel,
        out_shape=(
            jax.ShapeDtypeStruct((OWN, SIDE, SIDE), jnp.bfloat16),
            jax.ShapeDtypeStruct((8, 128), jnp.float32),
        ),
        in_specs=[pl.BlockSpec(memory_space=pltpu.HBM)] * 9,
        out_specs=(vmem, vmem),
        scratch_shapes=held + buffers + labels + codes + sems + [dma((3,))]
+ [dma((9,))]
        + [pltpu.VMEM((MINE, SIDE, SIDE), jnp.bfloat16), pltpu.VMEM((N_MIC, SIDE, SIDE), jnp.bfloat16)] + f32,
        compiler_params=pltpu.CompilerParams(
            collective_id=0, has_side_effects=True, vmem_limit_bytes=32 << 20
        ),
        name="project",
    )(*[pltpu.with_memory_space_constraint(x, pltpu.HBM) for x in inputs])
    return (refined, scores[0, :MINE])


def solution(mesh):
    tiles, items = P(("mic", "bin"), None, None), P(("mic", "bin"))
    return jax.shard_map(
        body,
        mesh=mesh,
        in_specs=(tiles, P(None, ("mic", "bin")), items, items, P(), P(), P(), tiles),
        out_specs=(tiles, items),
        check_vma=False,
    )
```

```python
import math

import jax
import jax.numpy as jnp
import ml_dtypes
import numpy as np
from jax import lax
from jax.experimental import pallas as pl
from jax.experimental.pallas import tpu as pltpu
from jax.sharding import PartitionSpec as P

PRIOR_WEIGHT = 0.5
EPSILON = 1e-06
CONTRAST = 0.1
AMPLITUDE = math.sqrt(1.0 - CONTRAST * CONTRAST)
SIDE = 256
PIXELS = SIDE * SIDE
N_MIC, N_BIN, N_Z, N_Y = 8, 32, 8, 4
OWN, MINE = 8, 4
ROWS = 32
CTF_GROUPS = 64
DEPTHS = (64, 64, 64, 32, 32)
CHUNKS = len(DEPTHS)
STARTS = [sum(DEPTHS[:c]) for c in range(CHUNKS)]
HOP, PLANE, OWNER = 0, 1, 2
ORDER = (
    (HOP, 0, 1), (HOP, 1, 1), (HOP, 0, 2), (HOP, 1, 2), (HOP, 0, 3), (HOP, 2, 1),
    (HOP, 1, 3), (HOP, 0, 4), (HOP, 2, 2), (HOP, 1, 4), (PLANE, 0, 0), (HOP, 3, 1),
    (HOP, 2, 3), (PLANE, 1, 0), (HOP, 4, 1), (HOP, 3, 2), (HOP, 2, 4), (HOP, 4, 2),
    (HOP, 3, 3), (PLANE, 2, 0), (HOP, 4, 3), (HOP, 3, 4), (OWNER, 1, 0), (HOP, 4, 4),
    (PLANE, 3, 0), (OWNER, 0, 0), (PLANE, 4, 0), (OWNER, 2, 0), (OWNER, 3, 0), (OWNER, 4, 0),
)
LABELS_AT = (6, 7, 11, 12, 16, 19)
MESH = pl.DeviceIdType.MESH


def hartley():
    k = np.arange(SIDE)
    angles = (np.outer(k, k) % SIDE).astype(np.float32) * np.float32(2.0 * math.pi / SIDE)
    return ((np.cos(angles) + np.sin(angles)) / np.float32(math.sqrt(SIDE))).astype(ml_dtypes.bfloat16)


def code_of(bin_ref, place_ref, group_ref, j):
    return place_ref[bin_ref[j]] * CTF_GROUPS + group_ref[j] + 1


def lanes_of(values):
    lane = lax.broadcasted_iota(jnp.int32, (8, 128), 1)
    tile = jnp.zeros((8, 128), jnp.int32)
    for j, value in enumerate(values):
        tile = jnp.where(lane == j, value, tile)
    return tile


def transform(offset_ref, basis_ref, images_ref, spectra):
    r = lax.broadcasted_iota(jnp.int32, (SIDE, SIDE), 0)
    c = lax.broadcasted_iota(jnp.int32, (SIDE, SIDE), 1)

    def one_hot(mask):
        return jnp.where(mask, 1.0, 0.0).astype(jnp.bfloat16)

    def dot(a, b):
        return jnp.dot(a, b, preferred_element_type=jnp.float32).astype(jnp.bfloat16)

    for j in range(MINE):
        moved = dot(one_hot(c == ((r + offset_ref[0, j]) & (SIDE - 1))), images_ref[j])
        moved = dot(moved, one_hot(r == ((c + offset_ref[1, j]) & (SIDE - 1))))
        spectra[j] = dot(dot(basis_ref[...], moved), basis_ref[...])


def kernel(*refs):
    inputs, (out_ref, score_ref), scratch = refs[:9], refs[9:11], refs[20:]
    bin_ref, bin_place_ref, group_ref, offset_ref, focus_ref, damp_ref, basis_ref, images_ref, refs_ref = held = refs[11:20]
    lines, packs = scratch[:CHUNKS], scratch[CHUNKS : 2 * CHUNKS]
    planes, parcels = scratch[2 * CHUNKS : 3 * CHUNKS], scratch[3 * CHUNKS : 4 * CHUNKS]
    (line_label, pack_label, plane_label, parcel_label, mine_label, line_code, plane_code, mine_code,
     z_send, z_recv, y_send, y_recv, m_send, m_recv, zl_send, zl_recv, yl_send, yl_recv,
     ml_send, ml_recv, am_send, am_recv, ay_send, ay_recv, az_send, az_recv, code_sem,
     load_sem, spectra, owned, ctf, sums, total, row_scores, row, plane_scores, line_scores) = scratch[4 * CHUNKS :]
    mic, column = lax.axis_index("mic"), lax.axis_index("bin")
    z, y = column >> 2, column & (N_Y - 1)

    def at_z(d):
        return (mic, (((z + d) & (N_Z - 1)) << 2) + y)

    def at_y(d):
        return (mic, (z << 2) + ((y + d) & (N_Y - 1)))

    def at_mic(d):
        return ((mic + d) & (N_MIC - 1), column)

    def send(src, dst, send_sem, recv_sem, peer):
        copy = pltpu.make_async_remote_copy(
            src_ref=src, dst_ref=dst, send_sem=send_sem, recv_sem=recv_sem,
            device_id=peer, device_id_type=MESH,
        )
        copy.start()
        copies.append(copy)
        return copy

    copies = []
    loads = [
        pltpu.make_async_copy(src, dst, load_sem.at[n])
        for n, (src, dst) in enumerate(zip(inputs, held))
    ]
    for load in loads:
        load.start()
    peers = [at_z(d) for d in range(1, N_Z)] + [at_y(d) for d in range(1, N_Y)] + [at_mic(d) for d in range(1, N_MIC)]
    barrier = pltpu.get_barrier_semaphore()
    for peer in peers:
        pl.semaphore_signal(barrier, inc=1, device_id=peer, device_id_type=MESH)
    for load in loads[:8]:
        load.wait()
    transform(offset_ref, basis_ref, images_ref, spectra)
    for block in range(2):
        total[block, N_MIC] = jnp.zeros((ROWS, SIDE), jnp.float32)
    sums[...] = jnp.zeros_like(sums)
    pl.semaphore_wait(barrier, len(peers))


    hops, y_copies, m_copies = {}, {}, {}
    pick_line, pick_plane = [], []
    half = N_Z // 2

    def hop(c, h):
        line = lines[c]
        if h == 1:
            line[0:MINE] = spectra[:, STARTS[c] : STARTS[c] + DEPTHS[c], :]
        for way in range(2):
            if h > 1:
                hops[c, way, h - 1].wait_recv()
            src = (1 - h) % N_Z if way == 0 else h - 1
            dst = N_Z - h if way == 0 else h
            low, count = 0, MINE
            if h == half:
                low, count = (MINE // 2) * way, MINE // 2
            hops[c, way, h] = send(
                line.at[pl.ds(src * MINE + low, count)], line.at[pl.ds(dst * MINE + low, count)],
                z_send.at[c, way, h - 1], z_recv.at[c, way, h - 1], at_z(1 if way == 0 else N_Z - 1),
            )

    def choose_line():
        keys = [[jnp.int32(0)] * MINE for _ in range(N_Y)]
        counts = [jnp.int32(0)] * N_Y
        for t in range(N_Z * MINE):
            code = line_code[t // MINE, 0, t % MINE]
            owner = (code - 1) >> 9
            here = ((owner >> 2) & (N_Z - 1)) == z
            away = (owner - y) & (N_Y - 1)
            key = code * (N_Z * MINE) + t
            for d in range(N_Y):
                hit = here & (away == d)
                rank = jnp.where(hit, counts[d], MINE)
                counts[d] = counts[d] + jnp.where(hit, 1, 0)
                keys[d] = [jnp.where(rank == k, key, keys[d][k]) for k in range(MINE)]
        pick_line.extend([[key & (N_Z * MINE - 1) for key in keys[d]] for d in range(N_Y)])
        for d in range(N_Y):
            tile = lanes_of([key >> 5 for key in keys[d]])
            if d == 0:
                plane_label[0] = tile
            else:
                pack_label[d - 1] = tile

    def to_plane(c):
        for way in range(2):
            hops[c, way, half].wait_recv()
        for d in range(N_Y):
            for k in range(MINE):
                tile = lines[c][pick_line[d][k]]
                if d == 0:
                    planes[c][k] = tile
                else:
                    packs[c][(d - 1) * MINE + k] = tile
        for d in range(1, N_Y):
            y_copies[c, d] = send(
                packs[c].at[pl.ds((d - 1) * MINE, MINE)], planes[c].at[pl.ds((N_Y - d) * MINE, MINE)],
                y_send.at[c, d - 1], y_recv.at[c, d - 1], at_y(d),
            )

    def choose_plane():
        keys = [jnp.int32(0)] * N_MIC
        for s in range(N_Y * MINE):
            code = plane_code[s // MINE, 0, s % MINE]
            away = (((code - 1) >> 14) - mic) & (N_MIC - 1)
            away = jnp.where(code > 0, away, N_MIC)
            key = code * (N_Y * MINE) + s
            keys = [jnp.where(away == d, key, keys[d]) for d in range(N_MIC)]
        pick_plane.extend([key & (N_Y * MINE - 1) for key in keys])
        for d in range(N_MIC):
            tile = jnp.full((8, 128), keys[d] >> 4, jnp.int32)
            if d == 0:
                mine_label[0] = tile
            else:
                parcel_label[d - 1] = tile

    def to_owner(c):
        for d in range(1, N_Y):
            y_copies[c, d].wait_recv()
        rows = pl.ds(STARTS[c], DEPTHS[c])
        for d in range(N_MIC):
            tile = planes[c][pick_plane[d]]
            if d == 0:
                owned[0, rows, :] = tile
            else:
                parcels[c][d - 1] = tile
        for d in range(1, N_MIC):
            m_copies[c, d] = send(
                parcels[c].at[d - 1], owned.at[N_MIC - d, rows, :],
                m_send.at[c, d - 1], m_recv.at[c, d - 1], at_mic(d),
            )

    def place_of(s):
        return ((mine_code[s, 0, 0] - 1) >> 6) & (OWN - 1)
    def tables():
        slot = lax.broadcasted_iota(jnp.int32, (N_MIC, SIDE), 0)
        focus = jnp.zeros((N_MIC, SIDE), jnp.float32)
        damp = jnp.zeros((N_MIC, SIDE), jnp.float32)
        for s in range(N_MIC):
            group = (mine_code[s, 0, 0] - 1) & (CTF_GROUPS - 1)
            focus = jnp.where(slot == s, focus_ref[group], focus)
            damp = jnp.where(slot == s, damp_ref[group], damp)
        k = lax.broadcasted_iota(jnp.int32, (N_MIC, SIDE), 1)
        folded = jnp.minimum(k, SIDE - k).astype(jnp.float32) * (2.0 / SIDE)
        square = folded * folded
        sine, cosine = jnp.sin(focus * square), jnp.cos(focus * square)
        envelope = jnp.exp(-damp * square)
        row_sine = jnp.transpose(-sine * envelope)
        row_cosine = jnp.transpose(-cosine * envelope)
        col_sine = (AMPLITUDE * cosine - CONTRAST * sine) * envelope
        col_cosine = (AMPLITUDE * sine + CONTRAST * cosine) * envelope
        for s in range(N_MIC):
            ctf[s] = (
                row_sine[:, s : s + 1] * col_sine[s : s + 1, :]
                + row_cosine[:, s : s + 1] * col_cosine[s : s + 1, :]
            )
    def collect(start, depth, source, with_data):
        @pl.loop(0, N_MIC)
        def _(s):
            place = place_of(s)
            parts = [jnp.zeros((16, SIDE), jnp.float32)] * 3
            for low in range(start, start + depth, 16):
                rows = pl.ds(low, 16)
                predicted = ctf[s, rows, :] * source[place, rows, :].astype(jnp.float32)
                values = owned[s, rows, :].astype(jnp.float32)
                parts[0] = parts[0] + predicted * values
                parts[1] = parts[1] + predicted * predicted
                if with_data:
                    parts[2] = parts[2] + values * values
            for n in range(3 if with_data else 2):
                sums[s, n] += parts[n][:8] + parts[n][8:]
    def correlate():
        slot = lax.broadcasted_iota(jnp.int32, (N_MIC, 128), 0)
        means = []
        for n in range(3):
            mean = jnp.zeros((N_MIC, 128), jnp.float32)
            for s in range(N_MIC):
                mean = jnp.where(slot == s, jnp.sum(sums[s, n], keepdims=True), mean)
            means.append(mean / PIXELS)
        correlation = means[0] / jnp.sqrt((means[1] + EPSILON) * (means[2] + EPSILON))
        weight = 1.0 / (1.0 + jnp.exp(-SIDE * correlation))
        weight = weight.astype(jnp.bfloat16).astype(jnp.float32)
        weights = [jnp.where(mine_code[s, 0, 0] > 0, weight[s, 0], 0.0) for s in range(N_MIC)]
        return correlation, weights
    def chains():
        places = [place_of(s) for s in range(N_MIC)]
        before = []
        for s in range(N_MIC):
            index = jnp.int32(N_MIC)
            for other in range(s):
                index = jnp.where(places[other] == places[s], other, index)
            before.append(index)
        last = []
        for p in range(OWN):
            index = jnp.int32(N_MIC)
            for s in range(N_MIC):
                index = jnp.where(places[s] == p, s, index)
            last.append(index)
        return before, last

    def update(weights, source, low, high):
        @pl.loop(low, high)
        def _(i):
            rows = pl.ds(pl.multiple_of(i * ROWS, ROWS), ROWS)
            for s in range(N_MIC):
                table = ctf[s, rows, :]
                scaled = weights[s] * table
                term = (scaled * owned[s, rows, :].astype(jnp.float32)).astype(jnp.bfloat16).astype(jnp.float32)
                total[0, s] = term + total[0, before[s]]
                total[1, s] = scaled * table + total[1, before[s]]
            for p in range(OWN):
                top = total[0, last[p]] + PRIOR_WEIGHT * source[p, rows, :].astype(jnp.float32)
                out_ref[p, rows, :] = (top / (total[1, last[p]] + PRIOR_WEIGHT)).astype(jnp.bfloat16)

    def read_codes(labels, label, code, n):
        for copy in labels:
            copy.wait_recv()
        fetch = pltpu.make_async_copy(label.at[:, 0:1], code.at[:, 0:1], code_sem.at[n])
        fetch.start()
        return fetch

    owners_done = []
    for n, (kind, c, h) in enumerate(ORDER):
        if n == 3:
            line_label[0] = lanes_of([code_of(bin_ref, bin_place_ref, group_ref, j) for j in range(MINE)])
            line_labels = [
                send(line_label.at[0, 0:1], line_label.at[N_Z - d, 0:1], zl_send.at[d - 1], zl_recv.at[d - 1], at_z(d))
                for d in range(1, N_Z)
            ]
        if n == LABELS_AT[0]:
            fetch = read_codes(line_labels, line_label, line_code, 0)
        if n == LABELS_AT[1]:
            fetch.wait()
            choose_line()
            plane_labels = [
                send(pack_label.at[d - 1, 0:1], plane_label.at[N_Y - d, 0:1], yl_send.at[d - 1], yl_recv.at[d - 1], at_y(d))
                for d in range(1, N_Y)
            ]
        if n == LABELS_AT[2]:
            fetch = read_codes(plane_labels, plane_label, plane_code, 1)
        if n == LABELS_AT[3]:
            fetch.wait()
            choose_plane()
            mine_labels = [
                send(parcel_label.at[d - 1, 0:1], mine_label.at[N_MIC - d, 0:1], ml_send.at[d - 1], ml_recv.at[d - 1], at_mic(d))
                for d in range(1, N_MIC)
            ]
        if n == LABELS_AT[4]:
            fetch = read_codes(mine_labels, mine_label, mine_code, 2)
        if n == LABELS_AT[5]:
            fetch.wait()
            tables()
        if kind == HOP:
            hop(c, h)
        elif kind == PLANE:
            to_plane(c)
        else:
            to_owner(c)
            owners_done.append(c)
    before, last = chains()
    loads[8].wait()
    for c in owners_done:
        for d in range(1, N_MIC):
            m_copies[c, d].wait_recv()
        collect(STARTS[c], DEPTHS[c], refs_ref, True)

    _, weights = correlate()
    update(weights, refs_ref, 0, SIDE // ROWS)
    routed = len(copies)
    for s in range(N_MIC):
        for n in range(2):
            sums[s, n] = jnp.zeros((8, SIDE), jnp.float32)
    collect(0, SIDE, out_ref, False)
    correlation, weights = correlate()

    row_scores[...] = correlation
    row[0:1, :] = correlation[0:1, :]
    by_mic = [
        send(row_scores.at[d : d + 1], row.at[N_MIC - d : N_MIC - d + 1], am_send.at[d - 1], am_recv.at[d - 1], at_mic(d))
        for d in range(1, N_MIC)
    ]
    update(weights, out_ref, 0, SIDE // ROWS // 2)
    for copy in copies[:routed]:
        copy.wait_send()
    for copy in by_mic:
        copy.wait_recv()
    lane = lax.broadcasted_iota(jnp.int32, (8, 128), 1)
    of_mic = lax.broadcasted_iota(jnp.int32, (8, 128), 0)
    plane_scores[0:1, :] = jnp.sum(jnp.where(lane == of_mic, row[...], 0.0), axis=0, keepdims=True)
    by_y = [
        send(plane_scores.at[0:1], plane_scores.at[N_Y - d : N_Y - d + 1], ay_send.at[d - 1], ay_recv.at[d - 1], at_y(d))
        for d in range(1, N_Y)
    ]
    update(weights, out_ref, SIDE // ROWS // 2, SIDE // ROWS)
    for copy in by_y:
        copy.wait_recv()
    line_scores[0] = plane_scores[...]
    by_z = [
        send(plane_scores, line_scores.at[N_Z - d], az_send.at[d - 1], az_recv.at[d - 1], at_z(d))
        for d in range(1, N_Z)
    ]
    for copy in by_z:
        copy.wait_recv()
    scores = jnp.zeros((8, 128), jnp.float32)
    for j in range(MINE):
        owner = bin_place_ref[bin_ref[j]] >> 3
        away_z = ((owner >> 2) - z) & (N_Z - 1)
        away_y = (owner - y) & (N_Y - 1)
        away_mic = ((owner >> 5) - mic) & (N_MIC - 1)
        found = jnp.where(lane[0:1, :] == away_mic, line_scores[away_z, pl.ds(away_y, 1), :], 0.0)
        scores = jnp.where(lane == j, jnp.sum(found, keepdims=True), scores)
    score_ref[...] = scores
    for copy in copies[routed:]:
        copy.wait_send()


def body(images, offsets, ctf_group, particle_bin, bin_place, defocus, bfactor, references):
    inputs = (particle_bin, bin_place, ctf_group, offsets, defocus, bfactor, jnp.asarray(hartley()), images, references)
    held = [(pltpu.SMEM if n < 6 else pltpu.VMEM)(x.shape, x.dtype) for n, x in enumerate(inputs)]
    vmem = pl.BlockSpec(memory_space=pltpu.VMEM)
    buffers = [pltpu.VMEM((n, depth, SIDE), jnp.bfloat16)
               for n in (N_Z * MINE, (N_Y - 1) * MINE, N_Y * MINE, N_MIC - 1) for depth in DEPTHS]
    labels = [pltpu.VMEM((n, 8, 128), jnp.int32) for n in (N_Z, N_Y - 1, N_Y, N_MIC - 1, N_MIC)]
    codes = [pltpu.SMEM((n, 8, 128), jnp.int32) for n in (N_Z, N_Y, N_MIC)]
    dma = pltpu.SemaphoreType.DMA
    sems = [dma(shape) for shape in ((CHUNKS, 2, N_Z // 2), (CHUNKS, N_Y - 1), (CHUNKS, N_MIC - 1),
                                     (N_Z - 1,), (N_Y - 1,), (N_MIC - 1,),
                                     (N_MIC - 1,), (N_Y - 1,), (N_Z - 1,)) for _ in range(2)]
    f32 = [pltpu.VMEM(shape, jnp.float32) for shape in (
        (N_MIC, SIDE, SIDE), (N_MIC, 3, 8, SIDE), (2, N_MIC + 1, ROWS, SIDE),
        (N_MIC, 128), (N_MIC, 128), (N_Y, 128), (N_Z, N_Y, 128))]
    refined, scores = pl.pallas_call(
        kernel,
        out_shape=(
            jax.ShapeDtypeStruct((OWN, SIDE, SIDE), jnp.bfloat16),
            jax.ShapeDtypeStruct((8, 128), jnp.float32),
        ),
        in_specs=[pl.BlockSpec(memory_space=pltpu.HBM)] * 9,
        out_specs=(vmem, vmem),
        scratch_shapes=held + buffers + labels + codes + sems + [dma((3,))]
+ [dma((9,))]
        + [pltpu.VMEM((MINE, SIDE, SIDE), jnp.bfloat16), pltpu.VMEM((N_MIC, SIDE, SIDE), jnp.bfloat16)] + f32,
        compiler_params=pltpu.CompilerParams(
            collective_id=0, has_side_effects=True, vmem_limit_bytes=32 << 20
        ),
        name="project",
    )(*[pltpu.with_memory_space_constraint(x, pltpu.HBM) for x in inputs])
    return (refined, scores[0, :MINE])


def solution(mesh):
    tiles, items = P(("mic", "bin"), None, None), P(("mic", "bin"))
    return jax.shard_map(
        body,
        mesh=mesh,
        in_specs=(tiles, P(None, ("mic", "bin")), items, items, P(), P(), P(), tiles),
        out_specs=(tiles, items),
        check_vma=False,
    )
```

```python
import math

import jax
import jax.numpy as jnp
import ml_dtypes
import numpy as np
from jax import lax
from jax.experimental import pallas as pl
from jax.experimental.pallas import tpu as pltpu
from jax.sharding import PartitionSpec as P

PRIOR_WEIGHT = 0.5
EPSILON = 1e-06
CONTRAST = 0.1
AMPLITUDE = math.sqrt(1.0 - CONTRAST * CONTRAST)
SIDE = 256
PIXELS = SIDE * SIDE
N_MIC, N_BIN, N_Z, N_Y = 8, 32, 8, 4
OWN, MINE = 8, 4
ROWS = 32
CTF_GROUPS = 64
DEPTHS = (64, 64, 64, 32, 32)
CHUNKS = len(DEPTHS)
STARTS = [sum(DEPTHS[:c]) for c in range(CHUNKS)]
HOP, PLANE, OWNER = 0, 1, 2
ORDER = (
    (HOP, 0, 1), (HOP, 1, 1), (HOP, 0, 2), (HOP, 1, 2), (HOP, 0, 3), (HOP, 2, 1),
    (HOP, 1, 3), (HOP, 0, 4), (HOP, 2, 2), (HOP, 1, 4), (PLANE, 0, 0), (HOP, 3, 1),
    (HOP, 2, 3), (PLANE, 1, 0), (HOP, 4, 1), (HOP, 3, 2), (HOP, 2, 4), (HOP, 4, 2),
    (HOP, 3, 3), (PLANE, 2, 0), (HOP, 4, 3), (HOP, 3, 4), (OWNER, 1, 0), (HOP, 4, 4),
    (PLANE, 3, 0), (OWNER, 0, 0), (PLANE, 4, 0), (OWNER, 2, 0), (OWNER, 3, 0), (OWNER, 4, 0),
)
LABELS_AT = (6, 7, 11, 12, 16, 19)
MESH = pl.DeviceIdType.MESH


def hartley():
    k = np.arange(SIDE)
    angles = (np.outer(k, k) % SIDE).astype(np.float32) * np.float32(2.0 * math.pi / SIDE)
    return ((np.cos(angles) + np.sin(angles)) / np.float32(math.sqrt(SIDE))).astype(ml_dtypes.bfloat16)


def code_of(bin_ref, place_ref, group_ref, j):
    return place_ref[bin_ref[j]] * CTF_GROUPS + group_ref[j] + 1


def lanes_of(values):
    lane = lax.broadcasted_iota(jnp.int32, (8, 128), 1)
    tile = jnp.zeros((8, 128), jnp.int32)
    for j, value in enumerate(values):
        tile = jnp.where(lane == j, value, tile)
    return tile


def transform(offset_ref, basis_ref, images_ref, spectra):
    r = lax.broadcasted_iota(jnp.int32, (SIDE, SIDE), 0)
    c = lax.broadcasted_iota(jnp.int32, (SIDE, SIDE), 1)

    def one_hot(mask):
        return jnp.where(mask, 1.0, 0.0).astype(jnp.bfloat16)

    def dot(a, b):
        return jnp.dot(a, b, preferred_element_type=jnp.float32).astype(jnp.bfloat16)

    for j in range(MINE):
        moved = dot(one_hot(c == ((r + offset_ref[0, j]) & (SIDE - 1))), images_ref[j])
        moved = dot(moved, one_hot(r == ((c + offset_ref[1, j]) & (SIDE - 1))))
        spectra[j] = dot(dot(basis_ref[...], moved), basis_ref[...])


def kernel(*refs):
    inputs, (out_ref, score_ref), scratch = refs[:9], refs[9:11], refs[20:]
    bin_ref, bin_place_ref, group_ref, offset_ref, focus_ref, damp_ref, basis_ref, images_ref, refs_ref = held = refs[11:20]
    lines, packs = scratch[:CHUNKS], scratch[CHUNKS : 2 * CHUNKS]
    planes, parcels = scratch[2 * CHUNKS : 3 * CHUNKS], scratch[3 * CHUNKS : 4 * CHUNKS]
    (line_label, pack_label, plane_label, parcel_label, mine_label, line_code, plane_code, mine_code,
     z_send, z_recv, y_send, y_recv, m_send, m_recv, zl_send, zl_recv, yl_send, yl_recv,
     ml_send, ml_recv, am_send, am_recv, ay_send, ay_recv, az_send, az_recv, code_sem,
     load_sem, spectra, owned, ctf, sums, total, row_scores, row, plane_scores, line_scores) = scratch[4 * CHUNKS :]
    mic, column = lax.axis_index("mic"), lax.axis_index("bin")
    z, y = column >> 2, column & (N_Y - 1)

    def at_z(d):
        return (mic, (((z + d) & (N_Z - 1)) << 2) + y)

    def at_y(d):
        return (mic, (z << 2) + ((y + d) & (N_Y - 1)))

    def at_mic(d):
        return ((mic + d) & (N_MIC - 1), column)

    def send(src, dst, send_sem, recv_sem, peer):
        copy = pltpu.make_async_remote_copy(
            src_ref=src, dst_ref=dst, send_sem=send_sem, recv_sem=recv_sem,
            device_id=peer, device_id_type=MESH,
        )
        copy.start()
        copies.append(copy)
        return copy

    copies = []
    loads = [
        pltpu.make_async_copy(src, dst, load_sem.at[n])
        for n, (src, dst) in enumerate(zip(inputs, held))
    ]
    for load in loads:
        load.start()
    peers = [at_z(d) for d in range(1, N_Z)] + [at_y(d) for d in range(1, N_Y)] + [at_mic(d) for d in range(1, N_MIC)]
    barrier = pltpu.get_barrier_semaphore()
    for peer in peers:
        pl.semaphore_signal(barrier, inc=1, device_id=peer, device_id_type=MESH)
    for load in loads[:8]:
        load.wait()
    transform(offset_ref, basis_ref, images_ref, spectra)
    for block in range(2):
        total[block, N_MIC] = jnp.zeros((ROWS, SIDE), jnp.float32)
    sums[...] = jnp.zeros_like(sums)
    pl.semaphore_wait(barrier, len(peers))


    hops, y_copies, m_copies = {}, {}, {}
    pick_line, pick_plane = [], []
    half = N_Z // 2

    def hop(c, h):
        line = lines[c]
        if h == 1:
            line[0:MINE] = spectra[:, STARTS[c] : STARTS[c] + DEPTHS[c], :]
        for way in range(2):
            if h > 1:
                hops[c, way, h - 1].wait_recv()
            src = (1 - h) % N_Z if way == 0 else h - 1
            dst = N_Z - h if way == 0 else h
            low, count = 0, MINE
            if h == half:
                low, count = (MINE // 2) * way, MINE // 2
            hops[c, way, h] = send(
                line.at[pl.ds(src * MINE + low, count)], line.at[pl.ds(dst * MINE + low, count)],
                z_send.at[c, way, h - 1], z_recv.at[c, way, h - 1], at_z(1 if way == 0 else N_Z - 1),
            )

    def choose_line():
        keys = [[jnp.int32(0)] * MINE for _ in range(N_Y)]
        counts = [jnp.int32(0)] * N_Y
        for t in range(N_Z * MINE):
            code = line_code[t // MINE, 0, t % MINE]
            owner = (code - 1) >> 9
            here = ((owner >> 2) & (N_Z - 1)) == z
            away = (owner - y) & (N_Y - 1)
            key = code * (N_Z * MINE) + t
            for d in range(N_Y):
                hit = here & (away == d)
                rank = jnp.where(hit, counts[d], MINE)
                counts[d] = counts[d] + jnp.where(hit, 1, 0)
                keys[d] = [jnp.where(rank == k, key, keys[d][k]) for k in range(MINE)]
        pick_line.extend([[key & (N_Z * MINE - 1) for key in keys[d]] for d in range(N_Y)])
        for d in range(N_Y):
            tile = lanes_of([key >> 5 for key in keys[d]])
            if d == 0:
                plane_label[0] = tile
            else:
                pack_label[d - 1] = tile

    def to_plane(c):
        for way in range(2):
            hops[c, way, half].wait_recv()
        for d in range(N_Y):
            for k in range(MINE):
                tile = lines[c][pick_line[d][k]]
                if d == 0:
                    planes[c][k] = tile
                else:
                    packs[c][(d - 1) * MINE + k] = tile
        for d in range(1, N_Y):
            y_copies[c, d] = send(
                packs[c].at[pl.ds((d - 1) * MINE, MINE)], planes[c].at[pl.ds((N_Y - d) * MINE, MINE)],
                y_send.at[c, d - 1], y_recv.at[c, d - 1], at_y(d),
            )

    def choose_plane():
        keys = [jnp.int32(0)] * N_MIC
        for s in range(N_Y * MINE):
            code = plane_code[s // MINE, 0, s % MINE]
            away = (((code - 1) >> 14) - mic) & (N_MIC - 1)
            away = jnp.where(code > 0, away, N_MIC)
            key = code * (N_Y * MINE) + s
            keys = [jnp.where(away == d, key, keys[d]) for d in range(N_MIC)]
        pick_plane.extend([key & (N_Y * MINE - 1) for key in keys])
        for d in range(N_MIC):
            tile = jnp.full((8, 128), keys[d] >> 4, jnp.int32)
            if d == 0:
                mine_label[0] = tile
            else:
                parcel_label[d - 1] = tile

    def to_owner(c):
        for d in range(1, N_Y):
            y_copies[c, d].wait_recv()
        rows = pl.ds(STARTS[c], DEPTHS[c])
        for d in range(N_MIC):
            tile = planes[c][pick_plane[d]]
            if d == 0:
                owned[0, rows, :] = tile
            else:
                parcels[c][d - 1] = tile
        for d in range(1, N_MIC):
            m_copies[c, d] = send(
                parcels[c].at[d - 1], owned.at[N_MIC - d, rows, :],
                m_send.at[c, d - 1], m_recv.at[c, d - 1], at_mic(d),
            )

    def place_of(s):
        return ((mine_code[s, 0, 0] - 1) >> 6) & (OWN - 1)
    def tables():
        slot = lax.broadcasted_iota(jnp.int32, (N_MIC, SIDE), 0)
        focus = jnp.zeros((N_MIC, SIDE), jnp.float32)
        damp = jnp.zeros((N_MIC, SIDE), jnp.float32)
        for s in range(N_MIC):
            group = (mine_code[s, 0, 0] - 1) & (CTF_GROUPS - 1)
            focus = jnp.where(slot == s, focus_ref[group], focus)
            damp = jnp.where(slot == s, damp_ref[group], damp)
        k = lax.broadcasted_iota(jnp.int32, (N_MIC, SIDE), 1)
        folded = jnp.minimum(k, SIDE - k).astype(jnp.float32) * (2.0 / SIDE)
        square = folded * folded
        sine, cosine = jnp.sin(focus * square), jnp.cos(focus * square)
        envelope = jnp.exp(-damp * square)
        row_sine = jnp.transpose(-sine * envelope)
        row_cosine = jnp.transpose(-cosine * envelope)
        col_sine = (AMPLITUDE * cosine - CONTRAST * sine) * envelope
        col_cosine = (AMPLITUDE * sine + CONTRAST * cosine) * envelope
        for s in range(N_MIC):
            ctf[s] = (
                row_sine[:, s : s + 1] * col_sine[s : s + 1, :]
                + row_cosine[:, s : s + 1] * col_cosine[s : s + 1, :]
            )
    def collect(start, depth, source, with_data):
        @pl.loop(0, N_MIC)
        def _(s):
            place = place_of(s)
            parts = [jnp.zeros((16, SIDE), jnp.float32)] * 3
            for low in range(start, start + depth, 16):
                rows = pl.ds(low, 16)
                predicted = ctf[s, rows, :] * source[place, rows, :].astype(jnp.float32)
                values = owned[s, rows, :].astype(jnp.float32)
                parts[0] = parts[0] + predicted * values
                parts[1] = parts[1] + predicted * predicted
                if with_data:
                    parts[2] = parts[2] + values * values
            for n in range(3 if with_data else 2):
                sums[s, n] += parts[n][:8] + parts[n][8:]
    def correlate():
        slot = lax.broadcasted_iota(jnp.int32, (N_MIC, 128), 0)
        means = []
        for n in range(3):
            mean = jnp.zeros((N_MIC, 128), jnp.float32)
            for s in range(N_MIC):
                mean = jnp.where(slot == s, jnp.sum(sums[s, n], keepdims=True), mean)
            means.append(mean / PIXELS)
        return means[0] / jnp.sqrt((means[1] + EPSILON) * (means[2] + EPSILON))

    def weigh(correlation):
        weight = 1.0 / (1.0 + jnp.exp(-SIDE * correlation))
        weight = weight.astype(jnp.bfloat16).astype(jnp.float32)
        return [jnp.where(mine_code[s, 0, 0] > 0, weight[s, 0], 0.0) for s in range(N_MIC)]
    def chains():
        places = [place_of(s) for s in range(N_MIC)]
        before = []
        for s in range(N_MIC):
            index = jnp.int32(N_MIC)
            for other in range(s):
                index = jnp.where(places[other] == places[s], other, index)
            before.append(index)
        last = []
        for p in range(OWN):
            index = jnp.int32(N_MIC)
            for s in range(N_MIC):
                index = jnp.where(places[s] == p, s, index)
            last.append(index)
        return before, last

    def update(weights, source, low, high):
        @pl.loop(low, high)
        def _(i):
            rows = pl.ds(pl.multiple_of(i * ROWS, ROWS), ROWS)
            for s in range(N_MIC):
                table = ctf[s, rows, :]
                scaled = weights[s] * table
                term = (scaled * owned[s, rows, :].astype(jnp.float32)).astype(jnp.bfloat16).astype(jnp.float32)
                total[0, s] = term + total[0, before[s]]
                total[1, s] = scaled * table + total[1, before[s]]
            for p in range(OWN):
                top = total[0, last[p]] + PRIOR_WEIGHT * source[p, rows, :].astype(jnp.float32)
                out_ref[p, rows, :] = (top / (total[1, last[p]] + PRIOR_WEIGHT)).astype(jnp.bfloat16)

    def read_codes(labels, label, code, n):
        for copy in labels:
            copy.wait_recv()
        fetch = pltpu.make_async_copy(label.at[:, 0:1], code.at[:, 0:1], code_sem.at[n])
        fetch.start()
        return fetch

    owners_done = []
    for n, (kind, c, h) in enumerate(ORDER):
        if n == 3:
            line_label[0] = lanes_of([code_of(bin_ref, bin_place_ref, group_ref, j) for j in range(MINE)])
            line_labels = [
                send(line_label.at[0, 0:1], line_label.at[N_Z - d, 0:1], zl_send.at[d - 1], zl_recv.at[d - 1], at_z(d))
                for d in range(1, N_Z)
            ]
        if n == LABELS_AT[0]:
            fetch = read_codes(line_labels, line_label, line_code, 0)
        if n == LABELS_AT[1]:
            fetch.wait()
            choose_line()
            plane_labels = [
                send(pack_label.at[d - 1, 0:1], plane_label.at[N_Y - d, 0:1], yl_send.at[d - 1], yl_recv.at[d - 1], at_y(d))
                for d in range(1, N_Y)
            ]
        if n == LABELS_AT[2]:
            fetch = read_codes(plane_labels, plane_label, plane_code, 1)
        if n == LABELS_AT[3]:
            fetch.wait()
            choose_plane()
            mine_labels = [
                send(parcel_label.at[d - 1, 0:1], mine_label.at[N_MIC - d, 0:1], ml_send.at[d - 1], ml_recv.at[d - 1], at_mic(d))
                for d in range(1, N_MIC)
            ]
        if n == LABELS_AT[4]:
            fetch = read_codes(mine_labels, mine_label, mine_code, 2)
        if n == LABELS_AT[5]:
            fetch.wait()
            tables()
        if kind == HOP:
            hop(c, h)
        elif kind == PLANE:
            to_plane(c)
        else:
            to_owner(c)
            owners_done.append(c)
    before, last = chains()
    loads[8].wait()
    for c in owners_done:
        for d in range(1, N_MIC):
            m_copies[c, d].wait_recv()
        collect(STARTS[c], DEPTHS[c], refs_ref, True)

    update(weigh(correlate()), refs_ref, 0, SIDE // ROWS)
    routed = len(copies)
    for s in range(N_MIC):
        for n in range(2):
            sums[s, n] = jnp.zeros((8, SIDE), jnp.float32)
    collect(0, SIDE, out_ref, False)
    correlation = correlate()

    row_scores[...] = correlation
    row[0:1, :] = correlation[0:1, :]
    by_mic = [
        send(row_scores.at[d : d + 1], row.at[N_MIC - d : N_MIC - d + 1], am_send.at[d - 1], am_recv.at[d - 1], at_mic(d))
        for d in range(1, N_MIC)
    ]
    weights = weigh(correlation)
    update(weights, out_ref, 0, SIDE // ROWS // 2)
    for copy in copies[:routed]:
        copy.wait_send()
    for copy in by_mic:
        copy.wait_recv()
    lane = lax.broadcasted_iota(jnp.int32, (8, 128), 1)
    of_mic = lax.broadcasted_iota(jnp.int32, (8, 128), 0)
    plane_scores[0:1, :] = jnp.sum(jnp.where(lane == of_mic, row[...], 0.0), axis=0, keepdims=True)
    by_y = [
        send(plane_scores.at[0:1], plane_scores.at[N_Y - d : N_Y - d + 1], ay_send.at[d - 1], ay_recv.at[d - 1], at_y(d))
        for d in range(1, N_Y)
    ]
    update(weights, out_ref, SIDE // ROWS // 2, SIDE // ROWS)
    for copy in by_y:
        copy.wait_recv()
    line_scores[0] = plane_scores[...]
    by_z = [
        send(plane_scores, line_scores.at[N_Z - d], az_send.at[d - 1], az_recv.at[d - 1], at_z(d))
        for d in range(1, N_Z)
    ]
    for copy in by_z:
        copy.wait_recv()
    scores = jnp.zeros((8, 128), jnp.float32)
    for j in range(MINE):
        owner = bin_place_ref[bin_ref[j]] >> 3
        away_z = ((owner >> 2) - z) & (N_Z - 1)
        away_y = (owner - y) & (N_Y - 1)
        away_mic = ((owner >> 5) - mic) & (N_MIC - 1)
        found = jnp.where(lane[0:1, :] == away_mic, line_scores[away_z, pl.ds(away_y, 1), :], 0.0)
        scores = jnp.where(lane == j, jnp.sum(found, keepdims=True), scores)
    score_ref[...] = scores
    for copy in copies[routed:]:
        copy.wait_send()


def body(images, offsets, ctf_group, particle_bin, bin_place, defocus, bfactor, references):
    inputs = (particle_bin, bin_place, ctf_group, offsets, defocus, bfactor, jnp.asarray(hartley()), images, references)
    held = [(pltpu.SMEM if n < 6 else pltpu.VMEM)(x.shape, x.dtype) for n, x in enumerate(inputs)]
    vmem = pl.BlockSpec(memory_space=pltpu.VMEM)
    buffers = [pltpu.VMEM((n, depth, SIDE), jnp.bfloat16)
               for n in (N_Z * MINE, (N_Y - 1) * MINE, N_Y * MINE, N_MIC - 1) for depth in DEPTHS]
    labels = [pltpu.VMEM((n, 8, 128), jnp.int32) for n in (N_Z, N_Y - 1, N_Y, N_MIC - 1, N_MIC)]
    codes = [pltpu.SMEM((n, 8, 128), jnp.int32) for n in (N_Z, N_Y, N_MIC)]
    dma = pltpu.SemaphoreType.DMA
    sems = [dma(shape) for shape in ((CHUNKS, 2, N_Z // 2), (CHUNKS, N_Y - 1), (CHUNKS, N_MIC - 1),
                                     (N_Z - 1,), (N_Y - 1,), (N_MIC - 1,),
                                     (N_MIC - 1,), (N_Y - 1,), (N_Z - 1,)) for _ in range(2)]
    f32 = [pltpu.VMEM(shape, jnp.float32) for shape in (
        (N_MIC, SIDE, SIDE), (N_MIC, 3, 8, SIDE), (2, N_MIC + 1, ROWS, SIDE),
        (N_MIC, 128), (N_MIC, 128), (N_Y, 128), (N_Z, N_Y, 128))]
    refined, scores = pl.pallas_call(
        kernel,
        out_shape=(
            jax.ShapeDtypeStruct((OWN, SIDE, SIDE), jnp.bfloat16),
            jax.ShapeDtypeStruct((8, 128), jnp.float32),
        ),
        in_specs=[pl.BlockSpec(memory_space=pltpu.HBM)] * 9,
        out_specs=(vmem, vmem),
        scratch_shapes=held + buffers + labels + codes + sems + [dma((3,))]
+ [dma((9,))]
        + [pltpu.VMEM((MINE, SIDE, SIDE), jnp.bfloat16), pltpu.VMEM((N_MIC, SIDE, SIDE), jnp.bfloat16)] + f32,
        compiler_params=pltpu.CompilerParams(
            collective_id=0, has_side_effects=True, vmem_limit_bytes=32 << 20
        ),
        name="project",
    )(*[pltpu.with_memory_space_constraint(x, pltpu.HBM) for x in inputs])
    return (refined, scores[0, :MINE])


def solution(mesh):
    tiles, items = P(("mic", "bin"), None, None), P(("mic", "bin"))
    return jax.shard_map(
        body,
        mesh=mesh,
        in_specs=(tiles, P(None, ("mic", "bin")), items, items, P(), P(), P(), tiles),
        out_specs=(tiles, items),
        check_vma=False,
    )
```
